32 devices in a mesh: seq: 4 (over z), ep: 8 (over y, x, core).
Axes of the slice: x: 2, y: 2, z: 4, core: 2. Of those that a mesh axis runs over, the one named last changes fastest.
Arguments:
- tokens: bfloat16 [4096, 2048], P(('seq', 'ep')), may hold values from -60 to 60
- expert_ids: int32 [4096, 8], P(('seq', 'ep')), may hold values from 0 to 31, all different within a row; in each aligned block of 128 rows (0 to 127, 128 to 255, ...) at most 48 rows name the same one
- route_weights: float32 [4096, 8], P(('seq', 'ep')), may hold values from 0.05 to 0.45
- norm_gain: float32 [2048], replicated, may hold values from 0.1 to 1.9
- gate_proj: bfloat16 [32, 2048, 768], P(('seq', 'ep')), may hold values from -0.125 to 0.125
- up_proj: bfloat16 [32, 2048, 768], P(('seq', 'ep')), may hold values from -0.125 to 0.125
- down_proj: bfloat16 [32, 768, 2048], P(('seq', 'ep')), may hold values from -0.21875 to 0.21875
- out_grad: bfloat16 [4096, 2048], P(('seq', 'ep')), may hold values from -6 to 6
Outputs:
- moe_out: bfloat16 [4096, 2048], P(('seq', 'ep'))
- in_grad: bfloat16 [4096, 2048], P(('seq', 'ep'))
The draws below stay inside these ranges and needn't reach their ends.
Inputs may be any that keep to these rules, and one draw needn't show every extreme that they name: `expert_ids`: in the rows of one device no expert is named more than 48 times, and in every draw some device names some expert exactly 48 times.
All inputs are finite; a program needn't handle non-finite values.
Results may differ from the reference program's by a relative error of at most 0.0071.
Values may be sent and summed in bfloat16 or wider, within the bound.
No kernel may reach another device: no remote copies, remote signals or barrier semaphores. Data moves between devices by JAX's collectives and lax.ppermute only.
A program may use at most 192 MiB of HBM per device.

```python
import math
import jax
import jax.numpy as jnp
import numpy as np
from jax import lax

D = 2048
FF = 768
TOP = 8
TOK_DEV = 128
EXPERTS = 32
TOKENS = 4096
CAP = 48
N_SEQ = 4
N_EP = 8


def draw_tokens(key, part):
    base_key, row_key, column_key = jax.random.split(key, 3)
    entries = jnp.clip(jax.random.normal(base_key, (TOKENS, D), jnp.float32), -6.0, 6.0)
    row_scale = jnp.exp(jax.random.uniform(row_key, (TOKENS, 1), jnp.float32, 0.0, math.log(10.0)))
    column_scale = jnp.exp(jax.random.uniform(column_key, (1, D), jnp.float32, 0.0, math.log(10.0)))
    return (0.1 * entries * row_scale * column_scale).astype(jnp.bfloat16)


def block_levels(key, shape, cuts, low, high):
    factor_of = 1.0
    for dim, shards_of in cuts:
        draws = jax.random.uniform(jax.random.fold_in(jax.random.fold_in(key, 6), dim), (shards_of,), jnp.float32, low / len(cuts), high / len(cuts))
        factor_of = factor_of * jnp.repeat(jnp.exp(draws), shape[dim] // shards_of).reshape((-1,) + (1,) * (len(shape) - 1 - dim))
    return factor_of


def deal_out(own_key, own, number, rows, amount, top, bound, slope):
    sequence = jax.random.permutation(own_key, amount)
    packed, usual = shares(amount, rows * top, bound, slope, True), shares(amount, rows * top, bound, slope, False)
    places = jnp.arange(amount)

    def named(sizes, rotation):
        used = int((sizes > 0).sum())
        fixed = max(1, used // 4)
        shifted = fixed + (places - fixed + rotation * (used - fixed)) % max(1, amount - fixed)
        return jnp.zeros((amount,), jnp.int32).at[sequence[jnp.where(places < fixed, places, shifted)]].set(jnp.asarray(sizes, jnp.int32))

    sizes = jnp.where(number % 4 == 0, named(packed, number // 4), named(usual, number - number // 4 - 1))
    mixed = jax.random.permutation(jax.random.fold_in(own, 3), amount)
    giver, taker = mixed[0:amount // 2 * 2:2], mixed[1:amount // 2 * 2:2]
    slack = jnp.minimum(sizes[giver] - 1, bound - sizes[taker]) // 2
    slack = jnp.where((giver == sequence[0]) | (taker == sequence[0]) | (sizes[taker] == 0), 0, jnp.maximum(slack, 0))
    shifted = jax.random.randint(jax.random.fold_in(own, 4), (amount // 2,), 0, 1 << 20) % (slack + 1)
    sizes = sizes.at[giver].add(-shifted).at[taker].add(shifted)
    members = jnp.searchsorted(jnp.cumsum(sizes), jnp.arange(rows * top), side="right").astype(jnp.int32)
    grid = members.reshape(top, rows).T
    grid = grid[jax.random.permutation(jax.random.fold_in(own, 1), rows)]
    rotation = jax.random.randint(jax.random.fold_in(own, 2), (rows, 1), 0, top)
    return jnp.take_along_axis(grid, (jnp.arange(top)[None, :] + rotation) % top, axis=1)


def shares(number_of, total, limit, slope, full):
    weights = [(1 << 20) // math.isqrt(standing ** slope) + 1 for standing in range(1, number_of + 1)]
    largest = limit if full else min(limit, max(-(-total // number_of), total * weights[0] // sum(weights)))
    least = 1 if total - largest >= number_of - 1 else 0
    holding, spare = [largest] + [least] * (number_of - 1), total - largest - least * (number_of - 1)
    while spare > 0:
        movable = [i for i in range(1, number_of) if holding[i] < largest] or [i for i in range(1, number_of) if holding[i] < limit]
        pool, budget = sum([weights[i] for i in movable]), spare
        for i in movable:
            extra = min(limit - holding[i], max(1, budget * weights[i] // pool), spare)
            holding[i] = holding[i] + extra
            spare = spare - extra
    return np.array(holding)


def bell_draw(rng, dims, deviation, bound, shards=(), kind=jnp.bfloat16):
    level = block_levels(rng, dims, shards, -0.22, 0.18) if shards else 1.0
    drawn = jax.random.normal(rng, dims, jnp.float32) * deviation * level
    return jnp.minimum(jnp.maximum(drawn, -bound), bound).astype(kind)


def setup_inputs(seed: int = 0) -> dict:
    keys = jax.random.split(jax.random.key(seed), 9)
    tokens = draw_tokens(jax.random.fold_in(keys[8], 71), 0)
    expert_ids_keys = jax.random.split(jax.random.fold_in(keys[1], 1), TOKENS // TOK_DEV)
    expert_ids_turns = jax.random.permutation(jax.random.fold_in(keys[1], 3), TOKENS // TOK_DEV)
    expert_ids = jax.vmap(lambda own, number: deal_out(jax.random.fold_in(keys[1], 2), own, number, TOK_DEV, EXPERTS, TOP, CAP, 2))(expert_ids_keys, expert_ids_turns).reshape((TOKENS, TOP))
    route_weights = jnp.clip(0.05 + 0.39999999 * jax.random.uniform(keys[2], (TOKENS, TOP), jnp.float32) ** block_levels(keys[2], (TOKENS, TOP), ((0, 32),), -0.2, 0.2), 0.05, 0.45)
    norm_gain = jnp.clip(1.0 + 0.18 * jax.random.normal(keys[3], (D,), jnp.float32), 0.1, 1.9)
    gate_proj = bell_draw(keys[4], (EXPERTS, D, FF), D ** -0.5, 0.125, ((0, 32),))
    up_proj = bell_draw(keys[5], (EXPERTS, D, FF), D ** -0.5, 0.125, ((0, 32),))
    down_proj = bell_draw(keys[6], (EXPERTS, FF, D), FF ** -0.5, 0.21875, ((0, 32),))
    out_grad = bell_draw(keys[7], (TOKENS, D), 1.0, 6.0, ((0, 32),))
    return {"tokens": tokens, "expert_ids": expert_ids, "route_weights": route_weights, "norm_gain": norm_gain, "gate_proj": gate_proj, "up_proj": up_proj, "down_proj": down_proj, "out_grad": out_grad}


EPS = 1e-06

def scale_rows(values, norm_gain):
    mean_square = lax.optimization_barrier(jnp.mean(values * values, axis=-1, keepdims=True))
    return values * lax.rsqrt(mean_square + EPS) * norm_gain

def expert_forward(inputs, gate_w, up_w, down_w):
    gate_act = jnp.dot(inputs, gate_w, preferred_element_type=jnp.float32)
    upward = jnp.dot(inputs, up_w, preferred_element_type=jnp.float32)
    hidden = (jax.nn.silu(gate_act) * upward).astype(jnp.bfloat16)
    result = jnp.dot(hidden, down_w, preferred_element_type=jnp.float32).astype(jnp.bfloat16)
    return (result, gate_act, upward)

def expert_backward(grads, gate_act, upward, gate_w, up_w, down_w):
    pairs = (((1,), (1,)), ((), ()))
    grad_hidden = lax.dot_general(grads, down_w, pairs, preferred_element_type=jnp.float32)
    sigmoid_gate = jax.nn.sigmoid(gate_act)
    grad_gate = (grad_hidden * upward * sigmoid_gate * (1.0 + gate_act * (1.0 - sigmoid_gate))).astype(jnp.bfloat16)
    grad_up = (grad_hidden * (gate_act * sigmoid_gate)).astype(jnp.bfloat16)
    summed = lax.dot_general(grad_gate, gate_w, pairs, preferred_element_type=jnp.float32)
    summed = summed + lax.dot_general(grad_up, up_w, pairs, preferred_element_type=jnp.float32)
    return summed.astype(jnp.bfloat16)

def block_ranks(block_ids):
    one_hot = (block_ids[:, None] == jnp.arange(EXPERTS, dtype=jnp.int32)[None, :]).astype(jnp.int32)
    earlier = jnp.cumsum(one_hot, axis=0) - one_hot
    return lax.optimization_barrier(jnp.sum(earlier * one_hot, axis=1)).astype(jnp.int32)

def reference(tokens, expert_ids, route_weights, norm_gain, gate_proj, up_proj, down_proj, out_grad):
    devices = N_SEQ * N_EP
    per_device = TOK_DEV * TOP
    x_float = tokens.astype(jnp.float32)
    normed = scale_rows(x_float, norm_gain).astype(jnp.bfloat16)
    flat_ids = expert_ids.reshape(-1).astype(jnp.int32)
    slot_rank = lax.map(block_ranks, flat_ids.reshape(devices, per_device)).reshape(-1).astype(jnp.int32)
    owners = jnp.arange(TOKENS * TOP, dtype=jnp.int32) // per_device
    position = (owners * CAP + slot_rank).astype(jnp.int32)
    slot_route = jnp.full((EXPERTS, devices * CAP), -1, dtype=jnp.int32)
    slot_route = slot_route.at[flat_ids, position].set(jnp.arange(TOKENS * TOP, dtype=jnp.int32))
    weights_flat = route_weights.reshape(-1)
    zero_value = jnp.zeros((), jnp.bfloat16)

    def visit(carry, member):
        out_sum, grad_sum = carry
        entries, gate_w, up_w, down_w = member
        filled = entries >= 0
        safe_route = jnp.maximum(entries, 0)
        source = (safe_route // TOP).astype(jnp.int32)
        inputs = jnp.where(filled[:, None], normed[source], zero_value)
        grads = jnp.where(filled[:, None], out_grad[source], zero_value)
        result, gate_act, upward = expert_forward(inputs, gate_w, up_w, down_w)
        grad_rows = expert_backward(grads, gate_act, upward, gate_w, up_w, down_w)
        factor = jnp.where(filled, weights_flat[safe_route], jnp.zeros((), weights_flat.dtype))[:, None]
        out_sum = out_sum.at[source].add(factor * result.astype(out_sum.dtype))
        grad_sum = grad_sum.at[source].add(factor * grad_rows.astype(grad_sum.dtype))
        return ((out_sum, grad_sum), None)
    start = (jnp.zeros((TOKENS, D), jnp.float32), jnp.zeros((TOKENS, D), jnp.float32))
    (out_sum, grad_sum), _ = lax.scan(visit, start, (slot_route, gate_proj, up_proj, down_proj))
    moe_out = out_sum.astype(jnp.bfloat16)

    def normalize(values):
        return scale_rows(values, norm_gain)
    _, pullback = jax.vjp(normalize, x_float)
    in_grad = pullback(grad_sum)[0].astype(jnp.bfloat16)
    return (moe_out, in_grad)
```

```python
import functools

import jax
import jax.numpy as jnp
from jax import lax
from jax.experimental import pallas as pl
from jax.experimental.pallas import tpu as pltpu
from jax.sharding import PartitionSpec as P

EPS = 1e-06
PAIRS = (((1,), (1,)), ((), ()))
BF16, F32 = jnp.bfloat16, jnp.float32


def scale_rows(values, norm_gain):
    mean_square = jnp.mean(values * values, axis=-1, keepdims=True)
    return values * lax.rsqrt(mean_square + EPS) * norm_gain


def norm_grad(x_float, norm_gain, grad):
    def normalize(values):
        return scale_rows(values, norm_gain)

    _, pullback = jax.vjp(normalize, x_float)
    return pullback(grad)[0].astype(BF16)


def slot_tables(index_ref, table_ref, onehot, factor, ranks, blocks, cap):
    tok = table_ref.shape[2]
    marks = jnp.concatenate(
        [jnp.where(table_ref[index_ref[b]] > 0.0, 1.0, 0.0).astype(BF16) for b in range(blocks)], axis=0
    )
    before = lax.broadcasted_iota(jnp.int32, (tok, tok), 0) < lax.broadcasted_iota(jnp.int32, (tok, tok), 1)
    ranks[...] = jnp.dot(marks, jnp.where(before, 1.0, 0.0).astype(BF16), preferred_element_type=F32)
    slots = lax.broadcasted_iota(jnp.int32, (cap, tok), 0).astype(F32)
    for b in range(blocks):
        weights = table_ref[index_ref[b]]
        for e in range(2):
            weight = weights[e : e + 1, :]
            rank = jnp.where(weight > 0.0, ranks[2 * b + e : 2 * b + e + 1, :], -1.0)
            hit = slots == rank
            onehot[b, e * cap : (e + 1) * cap, :] = jnp.where(hit, 1.0, 0.0).astype(BF16)
            slot_weight = jnp.sum(jnp.where(hit, weight, 0.0), axis=1, keepdims=True)
            factor[e, b * cap : (b + 1) * cap, :] = jnp.broadcast_to(slot_weight, (cap, tok))


def pick_rows(sources, onehot, rows, cap):
    for b, (ref, at) in enumerate(sources):
        tok = onehot.shape[2]
        picked = jnp.dot(onehot[b], ref[at * tok : (at + 1) * tok, :], preferred_element_type=F32).astype(BF16)
        rows[0, b * cap : (b + 1) * cap, :] = picked[:cap]
        rows[1, b * cap : (b + 1) * cap, :] = picked[cap:]


def put_rows(targets, onehot, rows, cap):
    tok = onehot.shape[2]
    for b, (ref, at) in enumerate(targets):
        both = jnp.concatenate([rows[0, b * cap : (b + 1) * cap, :], rows[1, b * cap : (b + 1) * cap, :]], axis=0)
        summed = lax.dot_general(onehot[b], both, (((0,), (0,)), ((), ())), preferred_element_type=F32)
        ref[at * tok : (at + 1) * tok, :] = summed.astype(BF16)


def scaled(total, factor):
    return (total * factor).astype(BF16)


def forward_kernel(cap, in_map, out_map, n_in, n_out, index_ref, *refs):
    table_ref = refs[0]
    ins = refs[1 : 1 + n_in]
    weights = refs[1 + n_in : 7 + n_in]
    outs = refs[7 + n_in : 7 + n_in + n_out]
    gate_ref, up_ref = refs[7 + n_in + n_out : 9 + n_in + n_out]
    onehot, factor, ranks, rows, total = refs[9 + n_in + n_out :]
    step = pl.program_id(0)
    tiles = pl.num_programs(0) // 2

    @pl.when(step == 0)
    def _():
        slot_tables(index_ref, table_ref, onehot, factor, ranks, len(in_map), cap)
        pick_rows([(ins[i], at) for i, at in in_map], onehot, rows, cap)

    def expert(e, gate_w, up_w, down_w):
        inputs = rows[e]
        gate_act = jnp.dot(inputs, gate_w[...], preferred_element_type=F32)
        upward = jnp.dot(inputs, up_w[...], preferred_element_type=F32)
        gate_ref[...] = gate_act
        up_ref[...] = upward
        hidden = (gate_act * jax.nn.sigmoid(gate_act) * upward).astype(BF16)
        part = jnp.dot(hidden, down_w[...], preferred_element_type=F32)

        @pl.when(step == e * tiles)
        def _():
            total[...] = part

        @pl.when(step > e * tiles)
        def _():
            total[...] += part

        @pl.when(step == (e + 1) * tiles - 1)
        def _():
            rows[e] = scaled(total[...], factor[e][:, :1])

    @pl.when(step < tiles)
    def _():
        expert(0, *weights[:3])

    @pl.when(step >= tiles)
    def _():
        expert(1, *weights[3:])

    @pl.when(step == 2 * tiles - 1)
    def _():
        put_rows([(outs[i], at) for i, at in out_map], onehot, rows, cap)


def backward_kernel(cap, in_map, out_map, n_in, n_out, index_ref, *refs):
    table_ref = refs[0]
    ins = refs[1 : 1 + n_in]
    weights = refs[1 + n_in : 7 + n_in]
    gate_ref, up_ref = refs[7 + n_in : 9 + n_in]
    outs = refs[9 + n_in : 9 + n_in + n_out]
    onehot, factor, ranks, rows, total = refs[9 + n_in + n_out :]
    step = pl.program_id(0)
    tiles = pl.num_programs(0) // 2

    @pl.when(step == 0)
    def _():
        slot_tables(index_ref, table_ref, onehot, factor, ranks, len(in_map), cap)
        pick_rows([(ins[i], at) for i, at in in_map], onehot, rows, cap)

    def expert(e, gate_w, up_w, down_w):
        grad_hidden = lax.dot_general(rows[e], down_w[...], PAIRS, preferred_element_type=F32)
        gate_act = gate_ref[...]
        sigmoid = jax.nn.sigmoid(gate_act)
        grad_gate = (grad_hidden * up_ref[...] * sigmoid * (1.0 + gate_act * (1.0 - sigmoid))).astype(BF16)
        grad_up = (grad_hidden * (gate_act * sigmoid)).astype(BF16)
        part = lax.dot_general(grad_gate, gate_w[...], PAIRS, preferred_element_type=F32)
        part = part + lax.dot_general(grad_up, up_w[...], PAIRS, preferred_element_type=F32)

        @pl.when(step == e * tiles)
        def _():
            total[...] = part

        @pl.when(step > e * tiles)
        def _():
            total[...] += part

        @pl.when(step == (e + 1) * tiles - 1)
        def _():
            rows[e] = scaled(total[...], factor[e][:, :1])

    @pl.when(step < tiles)
    def _():
        expert(0, *weights[:3])

    @pl.when(step >= tiles)
    def _():
        expert(1, *weights[3:])

    @pl.when(step == 2 * tiles - 1)
    def _():
        put_rows([(outs[i], at) for i, at in out_map], onehot, rows, cap)


def run_experts(kernel, index, table, ins, in_map, weights, acts, out_rows, out_map, cap):
    width = ins[0].shape[1]
    ff = weights[0].shape[1]
    tile = 256 if ff % 256 == 0 else ff
    tiles = ff // tile
    slots = len(in_map) * cap
    tok = table.shape[2]
    once = pl.Buffered(1)

    def whole(shape):
        return pl.BlockSpec(shape, lambda i, s: (0,) * len(shape), pipeline_mode=once)

    def columns(e):
        at = (lambda i: jnp.minimum(i, tiles - 1)) if e == 0 else (lambda i: jnp.maximum(i - tiles, 0))
        side = pl.BlockSpec((width, tile), lambda i, s: (0, at(i)))
        return [side, side, pl.BlockSpec((tile, width), lambda i, s: (at(i), 0))]

    act_spec = pl.BlockSpec((None, slots, tile), lambda i, s: (i // tiles, 0, i % tiles))
    in_specs = [whole(table.shape)] + [whole(a.shape) for a in ins] + columns(0) + columns(1)
    out_specs = [whole((r, width)) for r in out_rows]
    out_shape = [jax.ShapeDtypeStruct((r, width), BF16) for r in out_rows]
    operands = [index, table, *ins, *weights]
    if acts is None:
        out_specs += [act_spec] * 2
        out_shape += [jax.ShapeDtypeStruct((2, slots, ff), F32)] * 2
    else:
        in_specs += [act_spec] * 2
        operands += list(acts)
    return pl.pallas_call(
        functools.partial(kernel, cap, in_map, out_map, len(ins), len(out_rows)),
        out_shape=out_shape,
        grid_spec=pltpu.PrefetchScalarGridSpec(
            num_scalar_prefetch=1,
            grid=(2 * tiles,),
            in_specs=in_specs,
            out_specs=out_specs,
            scratch_shapes=[
                pltpu.VMEM((len(in_map), 2 * cap, tok), BF16),
                pltpu.VMEM((2, slots, tok), F32),
                pltpu.VMEM((2 * len(in_map), tok), F32),
                pltpu.VMEM((2, slots, width), BF16),
                pltpu.VMEM((slots, width), F32),
            ],
        ),
        compiler_params=pltpu.CompilerParams(
            dimension_semantics=("arbitrary",), vmem_limit_bytes=56 << 20
        ),
        cost_estimate=pl.CostEstimate(
            flops=2 * 2 * 3 * slots * width * ff,
            bytes_accessed=2 * (6 * width * ff + 2 * len(in_map) * tok * width) + 16 * slots * ff,
            transcendentals=2 * slots * ff,
        ),
    )(*operands)


def ep_permute(value, partner):
    return lax.ppermute(value, "ep", [(i, partner(i)) for i in range(8)])


def first(value):
    return ep_permute(value, lambda i: i ^ (4 if i & 1 else 2))


def second(value):
    return ep_permute(value, lambda i: i ^ (2 if i & 1 else 4))


def along_z(value, k):
    return lax.ppermute(value, "seq", [(i, i ^ k) for i in range(4)])


def spread(own):
    zs = [own] + [along_z(own, k) for k in (1, 2, 3)]
    arrays, names = [], []
    last0 = None
    for k in range(4):
        a = first(zs[k])
        if k == 1:
            b = along_z(last0, 1)
        else:
            b = second(jnp.concatenate([zs[k], a], axis=0))
            last0 = b if k == 0 else last0
        arrays += [zs[k], a, b]
        names += [[(k, 0)], [(k, 1)], [(k, 2), (k, 3)]]
    return arrays, names


def add(*values):
    total = values[0].astype(F32)
    for value in values[1:]:
        total = total + value.astype(F32)
    return total


def merge(near, far):
    tok = near[0].shape[0] // 2
    from_z = along_z(far[1], 1)
    sums = {}
    for k in (3, 2, 1, 0):
        part = near[k]
        if k != 1:
            send = far[k] if k else add(far[0], from_z).astype(BF16)
            got = second(send)
            other = add(part[tok:], got[tok:]).astype(BF16)
            mine = add(part[:tok], got[:tok])
        else:
            other = part[tok:]
            mine = part[:tok].astype(F32)
        mine = mine + first(other).astype(F32)
        sums[k] = along_z(mine.astype(BF16), k).astype(F32) if k else mine
    return sums[0] + sums[1] + sums[2] + sums[3]


def gathered(tokens, expert_ids, route_weights, norm_gain, gate_proj, up_proj, down_proj, out_grad):
    experts = lax.axis_size("seq") * lax.axis_size("ep")
    tok, fanout = expert_ids.shape
    cap = max(2, 3 * tok * fanout // (2 * experts))
    mine = (gate_proj[0], up_proj[0], down_proj[0])
    theirs = tuple(ep_permute(w, lambda i: i ^ 1) for w in mine)
    core = lax.axis_index("ep") % 2

    ids = jnp.arange(experts, dtype=jnp.int32)
    routes = jnp.sum(
        jnp.where(expert_ids[:, :, None] == ids[None, None, :], route_weights[:, :, None], 0.0), axis=1
    )
    pairs = routes.T.reshape(experts // 2, 2, tok)
    for_device = jnp.stack([pairs, pairs[:, ::-1]], axis=1).reshape(experts, 2 * tok)
    table = lax.all_to_all(for_device, ("seq", "ep"), split_axis=0, concat_axis=0, tiled=True)
    table = table.reshape(experts, 2, tok)

    x_float = tokens.astype(F32)
    normed = scale_rows(x_float, norm_gain).astype(BF16)
    x_arrays, x_names = spread(normed)
    g_arrays, _ = spread(out_grad)

    z, ep = lax.axis_index("seq"), lax.axis_index("ep")
    step_first = jnp.where(core == 1, 4, 2)
    step_second = jnp.where(core == 1, 2, 4)
    masks = [0, step_first, step_second, step_first | step_second]
    names = [n for group in x_names for n in group]
    index = jnp.stack([(z ^ k) * 8 + (ep ^ masks[j]) for k, j in names]).astype(jnp.int32)
    in_map = [(i, at) for i, group in enumerate(x_names) for at in range(len(group))]
    out_map = [(k if j < 2 else 4 + k, j % 2) for k, j in names]
    out_rows = [2 * tok] * 8

    results = run_experts(
        forward_kernel, index, table, x_arrays, in_map, mine + theirs, None, out_rows, out_map, cap
    )
    moe_out = merge(results[0:4], results[4:8]).astype(BF16)
    grads = run_experts(
        backward_kernel, index, table, g_arrays, in_map, mine + theirs, results[8:10], out_rows, out_map, cap
    )
    grad_normed = merge(grads[0:4], grads[4:8])
    return (moe_out, norm_grad(x_float, norm_gain, grad_normed))


def expert_forward(inputs, gate_w, up_w, down_w):
    gate_act = jnp.dot(inputs, gate_w, preferred_element_type=jnp.float32)
    upward = jnp.dot(inputs, up_w, preferred_element_type=jnp.float32)
    hidden = (jax.nn.silu(gate_act) * upward).astype(jnp.bfloat16)
    result = jnp.dot(hidden, down_w, preferred_element_type=jnp.float32).astype(jnp.bfloat16)
    return (result, gate_act, upward)


def expert_backward(grads, gate_act, upward, gate_w, up_w, down_w):
    pairs = (((1,), (1,)), ((), ()))
    grad_hidden = lax.dot_general(grads, down_w, pairs, preferred_element_type=jnp.float32)
    sigmoid_gate = jax.nn.sigmoid(gate_act)
    grad_gate = (
        grad_hidden * upward * sigmoid_gate * (1.0 + gate_act * (1.0 - sigmoid_gate))
    ).astype(jnp.bfloat16)
    grad_up = (grad_hidden * (gate_act * sigmoid_gate)).astype(jnp.bfloat16)
    summed = lax.dot_general(grad_gate, gate_w, pairs, preferred_element_type=jnp.float32)
    summed = summed + lax.dot_general(grad_up, up_w, pairs, preferred_element_type=jnp.float32)
    return summed.astype(jnp.bfloat16)


def move_out(slots):
    arrived = lax.all_to_all(slots, ("seq", "ep"), split_axis=0, concat_axis=0, tiled=True)
    return arrived


def move_back(slots):
    arrived = lax.all_to_all(slots, ("seq", "ep"), split_axis=0, concat_axis=0, tiled=True)
    return arrived


def run_live(compute, inputs):
    outputs = list(compute(inputs))
    return outputs


def exchanged(tokens, expert_ids, route_weights, norm_gain, gate_proj, up_proj, down_proj, out_grad):
    own_weights = (gate_proj[0], up_proj[0], down_proj[0])
    experts = lax.axis_size("seq") * lax.axis_size("ep")
    tok_count, fanout = expert_ids.shape
    model_width = tokens.shape[1]
    capacity = max(2, 3 * tok_count * fanout // (2 * experts))
    zero_value = jnp.zeros((), jnp.bfloat16)
    x_float = tokens.astype(jnp.float32)
    normed = scale_rows(x_float, norm_gain).astype(jnp.bfloat16)
    flat_ids = expert_ids.reshape(-1)
    one_hot = (flat_ids[:, None] == jnp.arange(experts, dtype=jnp.int32)[None, :]).astype(jnp.int32)
    slot_rank = jnp.sum((jnp.cumsum(one_hot, axis=0) - one_hot) * one_hot, axis=1)
    groups = [(0, capacity, own_weights)]
    position = flat_ids * capacity + slot_rank
    slot_route = (
        jnp.full((experts * capacity,), -1, jnp.int32)
        .at[position]
        .set(jnp.arange(flat_ids.shape[0], dtype=jnp.int32))
    )
    alive_slot = slot_route >= 0
    source = jnp.maximum(slot_route, 0) // fanout
    outgoing = jnp.where(alive_slot[:, None], normed[source], zero_value).reshape(
        experts, capacity, model_width
    )
    arrived = move_out(outgoing)
    first, width, weight_set = groups[0]
    inputs = arrived.reshape(-1, model_width)
    alive_rows = jnp.any(inputs != 0, axis=1)

    def forward_pass(parts, weight_set=weight_set):
        return expert_forward(parts[0], *weight_set)

    result, gate_act, upward = run_live(forward_pass, [inputs])
    saved = [(gate_act, upward, alive_rows)]
    result_parts = result.reshape(experts, width, model_width)
    route_out = move_back(result_parts).reshape(-1, model_width)[position]
    outgoing_grad = jnp.where(alive_slot[:, None], out_grad[source], zero_value).reshape(
        experts, capacity, model_width
    )
    grads_arrived = move_out(outgoing_grad)
    grad_parts = []
    for (first, width, weight_set), (gate_act, upward, alive_rows) in zip(groups, saved):
        grads = grads_arrived.reshape(-1, model_width)

        def backward_pass(parts, weight_set=weight_set):
            return (expert_backward(parts[0], parts[1], parts[2], *weight_set),)

        grad_rows = run_live(backward_pass, [grads, gate_act, upward])[0]
        grad_parts.append(grad_rows.reshape(experts, width, model_width))
    route_grad = move_back(grad_parts[0]).reshape(-1, model_width)[position]
    weight_cube = route_weights[:, :, None]
    moe_out = jnp.sum(
        weight_cube * route_out.reshape(tok_count, fanout, model_width).astype(jnp.float32), axis=1
    ).astype(jnp.bfloat16)
    grad_normed = jnp.sum(
        weight_cube * route_grad.reshape(tok_count, fanout, model_width).astype(jnp.float32), axis=1
    )

    def normalize(values):
        return scale_rows(values, norm_gain)

    _, pullback = jax.vjp(normalize, x_float)
    in_grad = pullback(grad_normed)[0].astype(jnp.bfloat16)
    return (moe_out, in_grad)


def solution(mesh):
    rows = P(("seq", "ep"), None)
    cubes = P(("seq", "ep"), None, None)
    planes = mesh.shape["seq"] == 4 and mesh.shape["ep"] == 8
    return jax.shard_map(
        gathered if planes else exchanged,
        mesh=mesh,
        in_specs=(rows, rows, rows, P(), cubes, cubes, cubes, rows),
        out_specs=(rows, rows),
        check_vma=False,
    )
```

```python
import functools

import jax
import jax.numpy as jnp
from jax import lax
from jax.experimental import pallas as pl
from jax.experimental.pallas import tpu as pltpu
from jax.sharding import PartitionSpec as P

EPS = 1e-06
PAIRS = (((1,), (1,)), ((), ()))
BF16, F32 = jnp.bfloat16, jnp.float32


def scale_rows(values, norm_gain):
    mean_square = jnp.mean(values * values, axis=-1, keepdims=True)
    return values * lax.rsqrt(mean_square + EPS) * norm_gain


def norm_grad(x_float, norm_gain, grad):
    def normalize(values):
        return scale_rows(values, norm_gain)

    _, pullback = jax.vjp(normalize, x_float)
    return pullback(grad)[0].astype(BF16)


def slot_tables(index_ref, table_ref, onehot, factor, ranks, blocks, cap):
    tok = table_ref.shape[2]
    marks = jnp.concatenate(
        [jnp.where(table_ref[index_ref[b]] > 0.0, 1.0, 0.0).astype(BF16) for b in range(blocks)], axis=0
    )
    before = lax.broadcasted_iota(jnp.int32, (tok, tok), 0) < lax.broadcasted_iota(jnp.int32, (tok, tok), 1)
    ranks[...] = jnp.dot(marks, jnp.where(before, 1.0, 0.0).astype(BF16), preferred_element_type=F32)
    slots = lax.broadcasted_iota(jnp.int32, (cap, tok), 0).astype(F32)
    for b in range(blocks):
        weights = table_ref[index_ref[b]]
        for e in range(2):
            weight = weights[e : e + 1, :]
            rank = jnp.where(weight > 0.0, ranks[2 * b + e : 2 * b + e + 1, :], -1.0)
            hit = slots == rank
            onehot[b, e * cap : (e + 1) * cap, :] = jnp.where(hit, 1.0, 0.0).astype(BF16)
            slot_weight = jnp.sum(jnp.where(hit, weight, 0.0), axis=1, keepdims=True)
            factor[e, b * cap : (b + 1) * cap, :] = jnp.broadcast_to(slot_weight, (cap, tok))


def pick_rows(sources, onehot, rows, cap):
    for b, (ref, at) in enumerate(sources):
        tok = onehot.shape[2]
        picked = jnp.dot(onehot[b], ref[at * tok : (at + 1) * tok, :], preferred_element_type=F32).astype(BF16)
        rows[0, b * cap : (b + 1) * cap, :] = picked[:cap]
        rows[1, b * cap : (b + 1) * cap, :] = picked[cap:]


def put_rows(targets, onehot, rows, cap):
    tok = onehot.shape[2]
    for b, (ref, at) in enumerate(targets):
        both = jnp.concatenate([rows[0, b * cap : (b + 1) * cap, :], rows[1, b * cap : (b + 1) * cap, :]], axis=0)
        summed = lax.dot_general(onehot[b], both, (((0,), (0,)), ((), ())), preferred_element_type=F32)
        ref[at * tok : (at + 1) * tok, :] = summed.astype(BF16)


def scaled(total, factor):
    return (total * factor).astype(BF16)


def forward_kernel(cap, in_map, out_map, n_in, n_out, index_ref, *refs):
    table_ref = refs[0]
    ins = refs[1 : 1 + n_in]
    weights = refs[1 + n_in : 7 + n_in]
    outs = refs[7 + n_in : 7 + n_in + n_out]
    gate_ref, up_ref = refs[7 + n_in + n_out : 9 + n_in + n_out]
    onehot, factor, ranks, rows, total = refs[9 + n_in + n_out :]
    step = pl.program_id(0)
    tiles = pl.num_programs(0) // 2

    @pl.when(step == 0)
    def _():
        slot_tables(index_ref, table_ref, onehot, factor, ranks, len(in_map), cap)
        pick_rows([(ins[i], at) for i, at in in_map], onehot, rows, cap)

    def expert(e, gate_w, up_w, down_w):
        inputs = rows[e]
        gate_act = jnp.dot(inputs, gate_w[...], preferred_element_type=F32)
        upward = jnp.dot(inputs, up_w[...], preferred_element_type=F32)
        gate_ref[...] = gate_act
        up_ref[...] = upward
        hidden = (gate_act * jax.nn.sigmoid(gate_act) * upward).astype(BF16)
        part = jnp.dot(hidden, down_w[...], preferred_element_type=F32)

        @pl.when(step == e * tiles)
        def _():
            total[...] = part

        @pl.when(step > e * tiles)
        def _():
            total[...] += part

        @pl.when(step == (e + 1) * tiles - 1)
        def _():
            rows[e] = scaled(total[...], factor[e][:, :1])

    @pl.when(step < tiles)
    def _():
        expert(0, *weights[:3])

    @pl.when(step >= tiles)
    def _():
        expert(1, *weights[3:])

    @pl.when(step == 2 * tiles - 1)
    def _():
        put_rows([(outs[i], at) for i, at in out_map], onehot, rows, cap)


def backward_kernel(cap, in_map, out_map, n_in, n_out, index_ref, *refs):
    table_ref = refs[0]
    ins = refs[1 : 1 + n_in]
    weights = refs[1 + n_in : 7 + n_in]
    gate_ref, up_ref = refs[7 + n_in : 9 + n_in]
    outs = refs[9 + n_in : 9 + n_in + n_out]
    onehot, factor, ranks, rows, total = refs[9 + n_in + n_out :]
    step = pl.program_id(0)
    tiles = pl.num_programs(0) // 2

    @pl.when(step == 0)
    def _():
        slot_tables(index_ref, table_ref, onehot, factor, ranks, len(in_map), cap)
        pick_rows([(ins[i], at) for i, at in in_map], onehot, rows, cap)

    def expert(e, gate_w, up_w, down_w):
        grad_hidden = lax.dot_general(rows[e], down_w[...], PAIRS, preferred_element_type=F32)
        gate_act = gate_ref[...]
        sigmoid = jax.nn.sigmoid(gate_act)
        grad_gate = (grad_hidden * up_ref[...] * sigmoid * (1.0 + gate_act * (1.0 - sigmoid))).astype(BF16)
        grad_up = (grad_hidden * (gate_act * sigmoid)).astype(BF16)
        part = lax.dot_general(grad_gate, gate_w[...], PAIRS, preferred_element_type=F32)
        part = part + lax.dot_general(grad_up, up_w[...], PAIRS, preferred_element_type=F32)

        @pl.when(step == e * tiles)
        def _():
            total[...] = part

        @pl.when(step > e * tiles)
        def _():
            total[...] += part

        @pl.when(step == (e + 1) * tiles - 1)
        def _():
            rows[e] = scaled(total[...], factor[e][:, :1])

    @pl.when(step < tiles)
    def _():
        expert(0, *weights[:3])

    @pl.when(step >= tiles)
    def _():
        expert(1, *weights[3:])

    @pl.when(step == 2 * tiles - 1)
    def _():
        put_rows([(outs[i], at) for i, at in out_map], onehot, rows, cap)


def run_experts(kernel, index, table, ins, in_map, weights, acts, out_rows, out_map, cap):
    width = ins[0].shape[1]
    ff = weights[0].shape[1]
    tile = 256 if ff % 256 == 0 else ff
    tiles = ff // tile
    slots = len(in_map) * cap
    tok = table.shape[2]
    once = pl.Buffered(1)

    def whole(shape):
        return pl.BlockSpec(shape, lambda i, s: (0,) * len(shape), pipeline_mode=once)

    def columns(e):
        at = (lambda i: jnp.minimum(i, tiles - 1)) if e == 0 else (lambda i: jnp.maximum(i - tiles, 0))
        side = pl.BlockSpec((width, tile), lambda i, s: (0, at(i)))
        return [side, side, pl.BlockSpec((tile, width), lambda i, s: (at(i), 0))]

    act_spec = pl.BlockSpec((None, slots, tile), lambda i, s: (i // tiles, 0, i % tiles))
    in_specs = [whole(table.shape)] + [whole(a.shape) for a in ins] + columns(0) + columns(1)
    out_specs = [whole((r, width)) for r in out_rows]
    out_shape = [jax.ShapeDtypeStruct((r, width), BF16) for r in out_rows]
    operands = [index, table, *ins, *weights]
    if acts is None:
        out_specs += [act_spec] * 2
        out_shape += [jax.ShapeDtypeStruct((2, slots, ff), F32)] * 2
    else:
        in_specs += [act_spec] * 2
        operands += list(acts)
    return pl.pallas_call(
        functools.partial(kernel, cap, in_map, out_map, len(ins), len(out_rows)),
        out_shape=out_shape,
        grid_spec=pltpu.PrefetchScalarGridSpec(
            num_scalar_prefetch=1,
            grid=(2 * tiles,),
            in_specs=in_specs,
            out_specs=out_specs,
            scratch_shapes=[
                pltpu.VMEM((len(in_map), 2 * cap, tok), BF16),
                pltpu.VMEM((2, slots, tok), F32),
                pltpu.VMEM((2 * len(in_map), tok), F32),
                pltpu.VMEM((2, slots, width), BF16),
                pltpu.VMEM((slots, width), F32),
            ],
        ),
        compiler_params=pltpu.CompilerParams(
            dimension_semantics=("arbitrary",), vmem_limit_bytes=56 << 20
        ),
        cost_estimate=pl.CostEstimate(
            flops=2 * 2 * 3 * slots * width * ff,
            bytes_accessed=2 * (6 * width * ff + 2 * len(in_map) * tok * width) + 16 * slots * ff,
            transcendentals=2 * slots * ff,
        ),
    )(*operands)


def ep_permute(value, partner):
    return lax.ppermute(value, "ep", [(i, partner(i)) for i in range(8)])


def first(value):
    return ep_permute(value, lambda i: i ^ (4 if i & 1 else 2))


def second(value):
    return ep_permute(value, lambda i: i ^ (2 if i & 1 else 4))


def along_z(value, k):
    return lax.ppermute(value, "seq", [(i, i ^ k) for i in range(4)])


def after(value, *others):
    return lax.optimization_barrier((value, *others))[0]


def both(near, far):
    return jnp.concatenate([near, far], axis=0)


def named(name, move, value, *args):
    with jax.named_scope(name):
        return move(value, *args)


def spread(x, g, weights, table):
    xs, gs = {}, {}
    xz, gz = {0: x}, {0: g}
    xs[0, 1] = named("x0a", first, x)
    xz[1] = named("x1z", along_z, x, 1)
    xz[2] = named("x2z", along_z, x, 2)
    gs[0, 1] = named("g0a", first, g)
    xs[0, 2] = named("x0b", second, both(x, xs[0, 1]))
    xz[3] = named("x3z", along_z, after(x, xz[1]), 3)
    xs[1, 1] = named("x1a", first, after(xz[1], gs[0, 1]))
    gs[0, 2] = named("g0b", second, both(g, after(gs[0, 1], xs[0, 2])))
    xs[1, 2] = named("x1b", along_z, after(xs[0, 2], xz[2]), 1)
    xs[2, 1] = named("x2a", first, after(xz[2], xs[1, 1], *weights, table))
    xs[2, 2] = named("x2b", second, both(xz[2], after(xs[2, 1], gs[0, 2])))
    gz[1] = named("g1z", along_z, after(g, xz[3]), 1)
    gz[2] = named("g2z", along_z, after(g, xz[3]), 2)
    xs[3, 1] = named("x3a", first, after(xz[3], xs[2, 1]))
    xs[3, 2] = named("x3b", second, both(xz[3], after(xs[3, 1], xs[2, 2])))
    gz[3] = named("g3z", along_z, after(g, gz[1], xs[1, 2]), 3)
    gs[1, 1] = named("g1a", first, after(gz[1], xs[3, 1]))
    gs[2, 1] = named("g2a", first, after(gz[2], gs[1, 1]))
    gs[1, 2] = named("g1b", along_z, after(gs[0, 2], gz[2]), 1)
    gs[2, 2] = named("g2b", second, both(gz[2], after(gs[2, 1], xs[3, 2])))
    gs[3, 1] = named("g3a", first, after(gz[3], gs[2, 1]))
    gs[3, 2] = named("g3b", second, both(gz[3], gs[3, 1]))
    for k in range(4):
        xs[k, 0], gs[k, 0] = xz[k], gz[k]
    keys = [(k, s) for k in range(4) for s in range(3)]
    names = [[(k, s)] if s < 2 else [(k, 2), (k, 3)] for k, s in keys]
    return [xs[i] for i in keys], [gs[i] for i in keys], names


def add(*values):
    total = values[0].astype(F32)
    for value in values[1:]:
        total = total + value.astype(F32)
    return total


def merge(near, far, tag, later=None):
    tok = near[0].shape[0] // 2
    got3 = named(tag + "3b", second, far[3])
    got2 = named(tag + "2b", second, far[2])
    from_z = named(tag + "1b", along_z, far[1], 1)
    got1 = named(tag + "1a", first, near[1][tok:])
    hold = (lambda v, *o: after(v, later, *o)) if later is not None else after
    send3 = add(hold(near[3][tok:]), got3[tok:]).astype(BF16)
    got3a = named(tag + "3a", first, send3)
    send2 = add(hold(near[2][tok:]), got2[tok:]).astype(BF16)
    got2a = named(tag + "2a", first, send2)
    sum3 = add(near[3][:tok], got3[:tok], got3a).astype(BF16)
    z3 = named(tag + "3z", along_z, sum3, 3)
    got0 = named(tag + "0b", second, add(far[0], hold(from_z)).astype(BF16))
    sum2 = add(near[2][:tok], got2[:tok], got2a).astype(BF16)
    z2 = named(tag + "2z", along_z, sum2, 2)
    sum1 = add(near[1][:tok], hold(got1)).astype(BF16)
    z1 = named(tag + "1z", along_z, sum1, 1)
    got0a = named(tag + "0a", first, add(near[0][tok:], got0[tok:]).astype(BF16))
    return add(near[0][:tok], got0[:tok], got0a, z1, z2, z3)


def gathered(tokens, expert_ids, route_weights, norm_gain, gate_proj, up_proj, down_proj, out_grad):
    experts = lax.axis_size("seq") * lax.axis_size("ep")
    tok, fanout = expert_ids.shape
    cap = max(2, 3 * tok * fanout // (2 * experts))
    mine = (gate_proj[0], up_proj[0], down_proj[0])
    theirs = tuple(named("swap", ep_permute, w, lambda i: i ^ 1) for w in mine)
    core = lax.axis_index("ep") % 2

    ids = jnp.arange(experts, dtype=jnp.int32)
    routes = jnp.sum(
        jnp.where(expert_ids[:, :, None] == ids[None, None, :], route_weights[:, :, None], 0.0), axis=1
    )
    pairs = routes.T.reshape(experts // 2, 2, tok)
    for_device = jnp.stack([pairs, pairs[:, ::-1]], axis=1).reshape(experts, 2 * tok)
    table = lax.all_to_all(for_device, ("seq", "ep"), split_axis=0, concat_axis=0, tiled=True)
    table = table.reshape(experts, 2, tok)

    x_float = tokens.astype(F32)
    normed = scale_rows(x_float, norm_gain).astype(BF16)
    x_arrays, g_arrays, x_names = spread(normed, out_grad, theirs, table)

    z, ep = lax.axis_index("seq"), lax.axis_index("ep")
    step_first = jnp.where(core == 1, 4, 2)
    step_second = jnp.where(core == 1, 2, 4)
    masks = [0, step_first, step_second, step_first | step_second]
    names = [n for group in x_names for n in group]
    index = jnp.stack([(z ^ k) * 8 + (ep ^ masks[j]) for k, j in names]).astype(jnp.int32)
    in_map = [(i, at) for i, group in enumerate(x_names) for at in range(len(group))]
    out_map = [(k if j < 2 else 4 + k, j % 2) for k, j in names]
    out_rows = [2 * tok] * 8

    results = run_experts(
        forward_kernel, index, table, x_arrays, in_map, mine + theirs, None, out_rows, out_map, cap
    )
    grads = run_experts(
        backward_kernel, index, table, g_arrays, in_map, mine + theirs, results[8:10], out_rows, out_map, cap
    )
    moe_out = merge(results[0:4], results[4:8], "o", grads[0]).astype(BF16)
    grad_normed = merge(grads[0:4], grads[4:8], "d")
    return (moe_out, norm_grad(x_float, norm_gain, grad_normed))


def expert_forward(inputs, gate_w, up_w, down_w):
    gate_act = jnp.dot(inputs, gate_w, preferred_element_type=jnp.float32)
    upward = jnp.dot(inputs, up_w, preferred_element_type=jnp.float32)
    hidden = (jax.nn.silu(gate_act) * upward).astype(jnp.bfloat16)
    result = jnp.dot(hidden, down_w, preferred_element_type=jnp.float32).astype(jnp.bfloat16)
    return (result, gate_act, upward)


def expert_backward(grads, gate_act, upward, gate_w, up_w, down_w):
    pairs = (((1,), (1,)), ((), ()))
    grad_hidden = lax.dot_general(grads, down_w, pairs, preferred_element_type=jnp.float32)
    sigmoid_gate = jax.nn.sigmoid(gate_act)
    grad_gate = (
        grad_hidden * upward * sigmoid_gate * (1.0 + gate_act * (1.0 - sigmoid_gate))
    ).astype(jnp.bfloat16)
    grad_up = (grad_hidden * (gate_act * sigmoid_gate)).astype(jnp.bfloat16)
    summed = lax.dot_general(grad_gate, gate_w, pairs, preferred_element_type=jnp.float32)
    summed = summed + lax.dot_general(grad_up, up_w, pairs, preferred_element_type=jnp.float32)
    return summed.astype(jnp.bfloat16)


def move_out(slots):
    arrived = lax.all_to_all(slots, ("seq", "ep"), split_axis=0, concat_axis=0, tiled=True)
    return arrived


def move_back(slots):
    arrived = lax.all_to_all(slots, ("seq", "ep"), split_axis=0, concat_axis=0, tiled=True)
    return arrived


def run_live(compute, inputs):
    outputs = list(compute(inputs))
    return outputs


def exchanged(tokens, expert_ids, route_weights, norm_gain, gate_proj, up_proj, down_proj, out_grad):
    own_weights = (gate_proj[0], up_proj[0], down_proj[0])
    experts = lax.axis_size("seq") * lax.axis_size("ep")
    tok_count, fanout = expert_ids.shape
    model_width = tokens.shape[1]
    capacity = max(2, 3 * tok_count * fanout // (2 * experts))
    zero_value = jnp.zeros((), jnp.bfloat16)
    x_float = tokens.astype(jnp.float32)
    normed = scale_rows(x_float, norm_gain).astype(jnp.bfloat16)
    flat_ids = expert_ids.reshape(-1)
    one_hot = (flat_ids[:, None] == jnp.arange(experts, dtype=jnp.int32)[None, :]).astype(jnp.int32)
    slot_rank = jnp.sum((jnp.cumsum(one_hot, axis=0) - one_hot) * one_hot, axis=1)
    groups = [(0, capacity, own_weights)]
    position = flat_ids * capacity + slot_rank
    slot_route = (
        jnp.full((experts * capacity,), -1, jnp.int32)
        .at[position]
        .set(jnp.arange(flat_ids.shape[0], dtype=jnp.int32))
    )
    alive_slot = slot_route >= 0
    source = jnp.maximum(slot_route, 0) // fanout
    outgoing = jnp.where(alive_slot[:, None], normed[source], zero_value).reshape(
        experts, capacity, model_width
    )
    arrived = move_out(outgoing)
    first, width, weight_set = groups[0]
    inputs = arrived.reshape(-1, model_width)
    alive_rows = jnp.any(inputs != 0, axis=1)

    def forward_pass(parts, weight_set=weight_set):
        return expert_forward(parts[0], *weight_set)

    result, gate_act, upward = run_live(forward_pass, [inputs])
    saved = [(gate_act, upward, alive_rows)]
    result_parts = result.reshape(experts, width, model_width)
    route_out = move_back(result_parts).reshape(-1, model_width)[position]
    outgoing_grad = jnp.where(alive_slot[:, None], out_grad[source], zero_value).reshape(
        experts, capacity, model_width
    )
    grads_arrived = move_out(outgoing_grad)
    grad_parts = []
    for (first, width, weight_set), (gate_act, upward, alive_rows) in zip(groups, saved):
        grads = grads_arrived.reshape(-1, model_width)

        def backward_pass(parts, weight_set=weight_set):
            return (expert_backward(parts[0], parts[1], parts[2], *weight_set),)

        grad_rows = run_live(backward_pass, [grads, gate_act, upward])[0]
        grad_parts.append(grad_rows.reshape(experts, width, model_width))
    route_grad = move_back(grad_parts[0]).reshape(-1, model_width)[position]
    weight_cube = route_weights[:, :, None]
    moe_out = jnp.sum(
        weight_cube * route_out.reshape(tok_count, fanout, model_width).astype(jnp.float32), axis=1
    ).astype(jnp.bfloat16)
    grad_normed = jnp.sum(
        weight_cube * route_grad.reshape(tok_count, fanout, model_width).astype(jnp.float32), axis=1
    )

    def normalize(values):
        return scale_rows(values, norm_gain)

    _, pullback = jax.vjp(normalize, x_float)
    in_grad = pullback(grad_normed)[0].astype(jnp.bfloat16)
    return (moe_out, in_grad)


def solution(mesh):
    rows = P(("seq", "ep"), None)
    cubes = P(("seq", "ep"), None, None)
    planes = mesh.shape["seq"] == 4 and mesh.shape["ep"] == 8
    return jax.shard_map(
        gathered if planes else exchanged,
        mesh=mesh,
        in_specs=(rows, rows, rows, P(), cubes, cubes, cubes, rows),
        out_specs=(rows, rows),
        check_vma=False,
    )
```

```python
import functools

import jax
import jax.numpy as jnp
from jax import lax
from jax.experimental import pallas as pl
from jax.experimental.pallas import tpu as pltpu
from jax.sharding import PartitionSpec as P

EPS = 1e-06
PAIRS = (((1,), (1,)), ((), ()))
BF16, F32 = jnp.bfloat16, jnp.float32


def scale_rows(values, norm_gain):
    mean_square = jnp.mean(values * values, axis=-1, keepdims=True)
    return values * lax.rsqrt(mean_square + EPS) * norm_gain


def norm_grad(x_float, norm_gain, grad):
    def normalize(values):
        return scale_rows(values, norm_gain)

    _, pullback = jax.vjp(normalize, x_float)
    return pullback(grad)[0].astype(BF16)


def slot_tables(index_ref, table_ref, onehot, factor, ranks, blocks, cap):
    tok = table_ref.shape[2]
    marks = jnp.concatenate(
        [jnp.where(table_ref[index_ref[b]] > 0.0, 1.0, 0.0).astype(BF16) for b in range(blocks)], axis=0
    )
    before = lax.broadcasted_iota(jnp.int32, (tok, tok), 0) < lax.broadcasted_iota(jnp.int32, (tok, tok), 1)
    ranks[...] = jnp.dot(marks, jnp.where(before, 1.0, 0.0).astype(BF16), preferred_element_type=F32)
    slots = lax.broadcasted_iota(jnp.int32, (cap, tok), 0).astype(F32)
    for b in range(blocks):
        weights = table_ref[index_ref[b]]
        for e in range(2):
            weight = weights[e : e + 1, :]
            rank = jnp.where(weight > 0.0, ranks[2 * b + e : 2 * b + e + 1, :], -1.0)
            hit = slots == rank
            onehot[b, e * cap : (e + 1) * cap, :] = jnp.where(hit, 1.0, 0.0).astype(BF16)
            slot_weight = jnp.sum(jnp.where(hit, weight, 0.0), axis=1, keepdims=True)
            factor[e, b * cap : (b + 1) * cap, :] = jnp.broadcast_to(slot_weight, (cap, tok))


def pick_rows(buffer, onehot, rows, blocks, cap):
    tok = onehot.shape[2]
    for b in blocks:
        picked = jnp.dot(onehot[b], buffer[b * tok : (b + 1) * tok, :], preferred_element_type=F32).astype(BF16)
        rows[0, b * cap : (b + 1) * cap, :] = picked[:cap]
        rows[1, b * cap : (b + 1) * cap, :] = picked[cap:]


def put_rows(buffer, onehot, rows, blocks, cap):
    tok = onehot.shape[2]
    for b in blocks:
        pair = jnp.concatenate([rows[0, b * cap : (b + 1) * cap, :], rows[1, b * cap : (b + 1) * cap, :]], axis=0)
        summed = lax.dot_general(onehot[b], pair, (((0,), (0,)), ((), ())), preferred_element_type=F32)
        buffer[b * tok : (b + 1) * tok, :] = summed.astype(BF16)


def tiles(size, most):
    step = most if size % most == 0 else size
    return [slice(at, at + step) for at in range(0, size, step)]


def forward_expert(e, rows, factor, gate_w, up_w, down_w, arrived, acts, keep, hidden):
    arrived("gate", e), arrived("up", e)
    for n in tiles(gate_w.shape[1], 256):
        gate_act = jnp.dot(rows[e], gate_w[:, n], preferred_element_type=F32)
        upward = jnp.dot(rows[e], up_w[:, n], preferred_element_type=F32)
        acts[0, :, n] = gate_act
        acts[1, :, n] = upward
        hidden[0, :, n] = (gate_act * jax.nn.sigmoid(gate_act) * upward).astype(BF16)
    keep(e)
    arrived("down", e)
    for n in tiles(down_w.shape[1], 512):
        total = jnp.dot(hidden[0], down_w[:, n], preferred_element_type=F32)
        rows[e, :, n] = (total * factor[e][:, :1]).astype(BF16)


def backward_expert(e, rows, factor, gate_w, up_w, down_w, arrived, acts, keep, hidden):
    arrived("down", e), keep(e)
    for n in tiles(gate_w.shape[1], 256):
        grad_hidden = lax.dot_general(rows[e], down_w[n, :], PAIRS, preferred_element_type=F32)
        gate_act = acts[0, :, n]
        sigmoid = jax.nn.sigmoid(gate_act)
        slope = sigmoid * (1.0 + gate_act * (1.0 - sigmoid))
        hidden[0, :, n] = (grad_hidden * acts[1, :, n] * slope).astype(BF16)
        hidden[1, :, n] = (grad_hidden * (gate_act * sigmoid)).astype(BF16)
    arrived("gate", e), arrived("up", e)
    for n in tiles(down_w.shape[1], 512):
        total = lax.dot_general(hidden[0], gate_w[n, :], PAIRS, preferred_element_type=F32)
        total = total + lax.dot_general(hidden[1], up_w[n, :], PAIRS, preferred_element_type=F32)
        rows[e, :, n] = (total * factor[e][:, :1]).astype(BF16)


def experts_kernel(forward, cap, groups, index_ref, *refs):
    count = len(groups)
    table_ref, ins, weights = refs[0], refs[1 : 1 + count], refs[1 + count : 7 + count]
    rest = refs[7 + count :]
    if forward:
        outs, kept, scratch = rest[:count], rest[count], rest[count + 1 :]
    else:
        kept, outs, scratch = rest[0], rest[1 : 1 + count], rest[1 + count :]
    buffer, rows, onehot, factor, ranks, sides, downs, acts, hidden, in_sem, weight_sem, act_sem = scratch
    tok = onehot.shape[2]
    blocks = sum(len(g) for g in groups)

    def window(i):
        return buffer.at[groups[i][0] * tok : (groups[i][-1] + 1) * tok]

    copies_in = [pltpu.make_async_copy(ins[i], window(i), in_sem.at[i]) for i in range(count)]
    held = {}
    for e in range(2):
        held["gate", e] = pltpu.make_async_copy(weights[3 * e], sides.at[2 * e], weight_sem.at[3 * e])
        held["up", e] = pltpu.make_async_copy(weights[3 * e + 1], sides.at[2 * e + 1], weight_sem.at[3 * e + 1])
        held["down", e] = pltpu.make_async_copy(weights[3 * e + 2], downs.at[e], weight_sem.at[3 * e + 2])
    if forward:
        copies_act = [pltpu.make_async_copy(acts.at[e], kept.at[e], act_sem.at[e]) for e in range(2)]
    else:
        copies_act = [pltpu.make_async_copy(kept.at[e], acts.at[e], act_sem.at[e]) for e in range(2)]
    for copy in copies_in:
        copy.start()
    for e in range(2):
        for name in ("gate", "up", "down") if forward else ("down", "gate", "up"):
            held[name, e].start()
        if not forward:
            copies_act[e].start()
    slot_tables(index_ref, table_ref, onehot, factor, ranks, blocks, cap)
    for copy, group in zip(copies_in, groups):
        copy.wait()
        pick_rows(buffer, onehot, rows, group, cap)
    for e in range(2):
        (forward_expert if forward else backward_expert)(
            e, rows, factor, sides.at[2 * e], sides.at[2 * e + 1], downs.at[e],
            lambda name, e: held[name, e].wait(), acts.at[e],
            lambda e: copies_act[e].start() if forward else copies_act[e].wait(), hidden,
        )
    copies_out = [pltpu.make_async_copy(window(i), outs[i], in_sem.at[i]) for i in range(count)]
    for copy, group in zip(copies_out, groups):
        put_rows(buffer, onehot, rows, group, cap)
        copy.start()
    for copy in copies_out:
        copy.wait()
    if forward:
        for copy in copies_act:
            copy.wait()


def run_experts(forward, index, table, ins, weights, acts, cap):
    width, ff, tok = ins[0].shape[1], weights[0].shape[1], table.shape[2]
    groups, blocks = [], 0
    for value in ins:
        groups.append(list(range(blocks, blocks + value.shape[0] // tok)))
        blocks += value.shape[0] // tok
    slots = blocks * cap
    kept = jax.ShapeDtypeStruct((2, 2, slots, ff), F32)
    out_shape = [jax.ShapeDtypeStruct(value.shape, BF16) for value in ins] + ([kept] if forward else [])
    in_place = pl.BlockSpec(memory_space=pl.ANY)
    operands = [index, table, *ins, *weights] + ([] if forward else [acts])
    return pl.pallas_call(
        functools.partial(experts_kernel, forward, cap, groups),
        out_shape=out_shape,
        in_specs=[pl.BlockSpec(memory_space=pltpu.SMEM), pl.BlockSpec(memory_space=pltpu.VMEM)]
        + [in_place] * (len(operands) - 2),
        out_specs=[in_place] * len(out_shape),
        scratch_shapes=[
            pltpu.VMEM((blocks * tok, width), BF16),
            pltpu.VMEM((2, slots, width), BF16),
            pltpu.VMEM((blocks, 2 * cap, tok), BF16),
            pltpu.VMEM((2, slots, tok), F32),
            pltpu.VMEM((2 * blocks, tok), F32),
            pltpu.VMEM((4, width, ff), BF16),
            pltpu.VMEM((2, ff, width), BF16),
            pltpu.VMEM((2, 2, slots, ff), F32),
            pltpu.VMEM((1 if forward else 2, slots, ff), BF16),
            pltpu.SemaphoreType.DMA((len(ins),)),
            pltpu.SemaphoreType.DMA((6,)),
            pltpu.SemaphoreType.DMA((2,)),
        ],
        compiler_params=pltpu.CompilerParams(vmem_limit_bytes=58 << 20),
        cost_estimate=pl.CostEstimate(
            flops=2 * 2 * 3 * slots * width * ff,
            bytes_accessed=2 * (6 * width * ff + 2 * blocks * tok * width) + 16 * slots * ff,
            transcendentals=2 * slots * ff,
        ),
    )(*operands)


def ep_permute(value, partner):
    return lax.ppermute(value, "ep", [(i, partner(i)) for i in range(8)])


def first(value):
    return ep_permute(value, lambda i: i ^ (4 if i & 1 else 2))


def second(value):
    return ep_permute(value, lambda i: i ^ (2 if i & 1 else 4))


def along_z(value, k):
    return lax.ppermute(value, "seq", [(i, i ^ k) for i in range(4)])


def add(*values):
    total = values[0].astype(F32)
    for value in values[1:]:
        total = total + value.astype(F32)
    return total


ORDER = (
    ("g0a", ()), ("x0a", ()), ("x2z", ()), ("x1z", ()), ("w0", ()), ("x0b", ("g0a",)), ("g0b", ("w0", "x0a",)),
    ("w2", ("w0", "x0a", "g0a",)), ("w1", ("w2",)), ("x3z", ("w2",)), ("x1a", ("x2z", "w2",)),
    ("x2a", ("w1", "x1z",)), ("x1b", ("w1", "x1z", "x2z",)), ("g2z", ("x3z", "x0b", "w1", "x1z",)),
    ("tab", ("g0b", "x3z", "x0b", "w1", "x1z",)), ("x3a", ("x1a", "g0b", "x0b", "w1",)),
    ("x2b", ("x1a", "g0b", "x3z", "x0b",)), ("x3b", ("x2a",)), ("g2a", ("x3a", "x2a",)),
    ("g3z", ("x3a", "x2a",)), ("g1z", ("x1b", "x2b", "g2z", "x3a",)), ("g2b", ("x1b", "x2b",)),
    ("F", ("g2a",)), ("o1a", ("g1z", "g2b", "g3z",)), ("g3a", ("F", "g1z", "g2b",)),
    ("o3b", ("g1z", "g2b", "g3z",)), ("g1b", ("F", "g1z", "g2b", "g3z",)), ("o1z", ()), ("g3b", ("o1a",)),
    ("o3a", ("g3a", "o1a",)), ("g1a", ("o3b", "g3a", "o1a",)), ("o2b", ("o1z", "o3b", "g3a",)),
    ("o1b", ("g1b", "o1z", "o3b", "g3a",)), ("o3z", ("g3b", "g1b", "o1z",)), ("B", ("o3a", "o1z",)),
    ("o2a", ("B", "o1b", "o3z",)), ("d3b", ("o1b", "o3z", "o2b",)), ("d2b", ("o1b", "o3z", "o2b",)),
    ("d1b", ("o1b", "o3z", "o2b",)), ("o2z", ()), ("d3a", ("o2a",)), ("d1a", ("d2b", "d3b", "o2a",)),
    ("d2a", ("d3a", "o2z",)), ("d3z", ("o2z", "d2b",)), ("d0b", ("d1a", "d3a", "o2z",)),
    ("o0b", ("d1b", "d1a", "d3a", "o2z",)), ("d2z", ("d1b", "d1a",)), ("d1z", ("d3z", "d2a", "d1b",)),
    ("d0a", ("d3z", "d2a",)), ("o0a", ("d0b", "d3z", "d2a",)),
)


def gathered(tokens, expert_ids, route_weights, norm_gain, gate_proj, up_proj, down_proj, out_grad):
    experts = lax.axis_size("seq") * lax.axis_size("ep")
    tok, fanout = expert_ids.shape
    cap = max(2, 3 * tok * fanout // (2 * experts))
    mine = (gate_proj[0], up_proj[0], down_proj[0])
    ids = jnp.arange(experts, dtype=jnp.int32)
    routes = jnp.sum(
        jnp.where(expert_ids[:, :, None] == ids[None, None, :], route_weights[:, :, None], 0.0), axis=1
    )
    pairs = routes.T.reshape(experts // 2, 2, tok)
    for_device = jnp.stack([pairs, pairs[:, ::-1]], axis=1).reshape(experts, 2 * tok)
    x_float = tokens.astype(F32)
    normed = scale_rows(x_float, norm_gain).astype(BF16)
    z, ep = lax.axis_index("seq"), lax.axis_index("ep")
    core = ep % 2
    step_first = jnp.where(core == 1, 4, 2)
    step_second = jnp.where(core == 1, 2, 4)
    masks = [0, step_first, step_second, step_first | step_second]
    done = {"x0": normed, "g0": out_grad}

    def experts_pass(forward, offsets, source, target, acts, wait):
        keys = [(k, s) for k in offsets for s in "0ab"]
        blocks = [(k, j) for k, s in keys for j in ((2, 3) if s == "b" else ("0a".index(s),))]
        index = jnp.stack([(z ^ k) * 8 + (ep ^ masks[j]) for k, j in blocks]).astype(jnp.int32)
        arrays = [done[source + ("0" if (k, s) == (0, "0") else f"{k}z" if s == "0" else f"{k}{s}")] for k, s in keys]
        theirs = tuple(done[f"w{i}"] for i in range(3))
        table = done["tab"].reshape(experts, 2, tok)
        out = run_experts(forward, wait(index), table, arrays, mine + theirs, acts, cap)
        for (k, s), value in zip(keys, out):
            done[f"{target}part{k}{s}"] = value
        return out

    def spread_step(name, wait):
        t, k, move = name[0], int(name[1]), name[2]
        own = done[f"{t}0"]
        if move == "z":
            return along_z(wait(done[f"{t}2z"]), 1) if k == 3 else along_z(wait(own), k)
        if name[1:] == "1b":
            return along_z(wait(done[f"{t}0b"]), 1)
        shard = own if k == 0 else done[f"{t}{k}z"]
        if move == "a":
            return first(wait(shard))
        return second(jnp.concatenate([shard, wait(done[f"{t}{k}a"])], axis=0))

    def merge_step(name, wait):
        t, k, move = name[0], int(name[1]), name[2]

        def part(s):
            return done[f"{t}part{k}{s}"]

        if name[1:] == "1b":
            return along_z(wait(part("b")), 1)
        if move == "b":
            value = add(part("b"), done[f"{t}1b"]).astype(BF16) if k == 0 else part("b")
            return second(wait(value))
        if move == "a":
            value = part("a") if k == 1 else add(part("a"), done[f"{t}{k}b"][tok:]).astype(BF16)
            return first(wait(value))
        value = total(t, k)
        return along_z(wait(value.astype(BF16)), 2 if k == 2 else 1)

    def total(t, k):
        values = [done[f"{t}part{k}0"], done[f"{t}{k}a"]]
        if k != 1:
            values.append(done[f"{t}{k}b"][:tok])
        if k == 2:
            values.append(done[f"{t}3z"])
        if k == 0:
            values += [done[f"{t}1z"], done[f"{t}2z"]]
        return add(*values)

    acts = {}
    for name, others in ORDER:

        def wait(value, others=others):
            if not others:
                return value
            return lax.optimization_barrier((value, *[done[n] for n in others]))[0]

        with jax.named_scope(name):
            if name[0] in "FB":
                offsets = {"0": (0, 2), "1": (1, 3)}.get(name[1:], (0, 1, 2, 3))
                if name[0] == "F":
                    out = experts_pass(True, offsets, "x", "o", None, wait)
                    acts[offsets] = out[-1]
                else:
                    out = experts_pass(False, offsets, "g", "d", acts[offsets], wait)
                done[name] = out[0]
            elif name == "tab":
                done[name] = lax.all_to_all(wait(for_device), ("seq", "ep"), split_axis=0, concat_axis=0, tiled=True)
            elif name[0] == "w":
                done[name] = ep_permute(wait(mine[int(name[1])]), lambda i: i ^ 1)
            else:
                done[name] = (spread_step if name[0] in "xg" else merge_step)(name, wait)
    return (total("o", 0).astype(BF16), norm_grad(x_float, norm_gain, total("d", 0)))


def expert_forward(inputs, gate_w, up_w, down_w):
    gate_act = jnp.dot(inputs, gate_w, preferred_element_type=jnp.float32)
    upward = jnp.dot(inputs, up_w, preferred_element_type=jnp.float32)
    hidden = (jax.nn.silu(gate_act) * upward).astype(jnp.bfloat16)
    result = jnp.dot(hidden, down_w, preferred_element_type=jnp.float32).astype(jnp.bfloat16)
    return (result, gate_act, upward)


def expert_backward(grads, gate_act, upward, gate_w, up_w, down_w):
    pairs = (((1,), (1,)), ((), ()))
    grad_hidden = lax.dot_general(grads, down_w, pairs, preferred_element_type=jnp.float32)
    sigmoid_gate = jax.nn.sigmoid(gate_act)
    grad_gate = (
        grad_hidden * upward * sigmoid_gate * (1.0 + gate_act * (1.0 - sigmoid_gate))
    ).astype(jnp.bfloat16)
    grad_up = (grad_hidden * (gate_act * sigmoid_gate)).astype(jnp.bfloat16)
    summed = lax.dot_general(grad_gate, gate_w, pairs, preferred_element_type=jnp.float32)
    summed = summed + lax.dot_general(grad_up, up_w, pairs, preferred_element_type=jnp.float32)
    return summed.astype(jnp.bfloat16)


def move_out(slots):
    arrived = lax.all_to_all(slots, ("seq", "ep"), split_axis=0, concat_axis=0, tiled=True)
    return arrived


def move_back(slots):
    arrived = lax.all_to_all(slots, ("seq", "ep"), split_axis=0, concat_axis=0, tiled=True)
    return arrived


def run_live(compute, inputs):
    outputs = list(compute(inputs))
    return outputs


def exchanged(tokens, expert_ids, route_weights, norm_gain, gate_proj, up_proj, down_proj, out_grad):
    own_weights = (gate_proj[0], up_proj[0], down_proj[0])
    experts = lax.axis_size("seq") * lax.axis_size("ep")
    tok_count, fanout = expert_ids.shape
    model_width = tokens.shape[1]
    capacity = max(2, 3 * tok_count * fanout // (2 * experts))
    zero_value = jnp.zeros((), jnp.bfloat16)
    x_float = tokens.astype(jnp.float32)
    normed = scale_rows(x_float, norm_gain).astype(jnp.bfloat16)
    flat_ids = expert_ids.reshape(-1)
    one_hot = (flat_ids[:, None] == jnp.arange(experts, dtype=jnp.int32)[None, :]).astype(jnp.int32)
    slot_rank = jnp.sum((jnp.cumsum(one_hot, axis=0) - one_hot) * one_hot, axis=1)
    groups = [(0, capacity, own_weights)]
    position = flat_ids * capacity + slot_rank
    slot_route = (
        jnp.full((experts * capacity,), -1, jnp.int32)
        .at[position]
        .set(jnp.arange(flat_ids.shape[0], dtype=jnp.int32))
    )
    alive_slot = slot_route >= 0
    source = jnp.maximum(slot_route, 0) // fanout
    outgoing = jnp.where(alive_slot[:, None], normed[source], zero_value).reshape(
        experts, capacity, model_width
    )
    arrived = move_out(outgoing)
    first, width, weight_set = groups[0]
    inputs = arrived.reshape(-1, model_width)
    alive_rows = jnp.any(inputs != 0, axis=1)

    def forward_pass(parts, weight_set=weight_set):
        return expert_forward(parts[0], *weight_set)

    result, gate_act, upward = run_live(forward_pass, [inputs])
    saved = [(gate_act, upward, alive_rows)]
    result_parts = result.reshape(experts, width, model_width)
    route_out = move_back(result_parts).reshape(-1, model_width)[position]
    outgoing_grad = jnp.where(alive_slot[:, None], out_grad[source], zero_value).reshape(
        experts, capacity, model_width
    )
    grads_arrived = move_out(outgoing_grad)
    grad_parts = []
    for (first, width, weight_set), (gate_act, upward, alive_rows) in zip(groups, saved):
        grads = grads_arrived.reshape(-1, model_width)

        def backward_pass(parts, weight_set=weight_set):
            return (expert_backward(parts[0], parts[1], parts[2], *weight_set),)

        grad_rows = run_live(backward_pass, [grads, gate_act, upward])[0]
        grad_parts.append(grad_rows.reshape(experts, width, model_width))
    route_grad = move_back(grad_parts[0]).reshape(-1, model_width)[position]
    weight_cube = route_weights[:, :, None]
    moe_out = jnp.sum(
        weight_cube * route_out.reshape(tok_count, fanout, model_width).astype(jnp.float32), axis=1
    ).astype(jnp.bfloat16)
    grad_normed = jnp.sum(
        weight_cube * route_grad.reshape(tok_count, fanout, model_width).astype(jnp.float32), axis=1
    )

    def normalize(values):
        return scale_rows(values, norm_gain)

    _, pullback = jax.vjp(normalize, x_float)
    in_grad = pullback(grad_normed)[0].astype(jnp.bfloat16)
    return (moe_out, in_grad)


def solution(mesh):
    rows = P(("seq", "ep"), None)
    cubes = P(("seq", "ep"), None, None)
    planes = mesh.shape["seq"] == 4 and mesh.shape["ep"] == 8
    return jax.shard_map(
        gathered if planes else exchanged,
        mesh=mesh,
        in_specs=(rows, rows, rows, P(), cubes, cubes, cubes, rows),
        out_specs=(rows, rows),
        check_vma=False,
    )
```

```python
import functools

import jax
import jax.numpy as jnp
from jax import lax
from jax.experimental import pallas as pl
from jax.experimental.pallas import tpu as pltpu
from jax.sharding import PartitionSpec as P

EPS = 1e-06
PAIRS = (((1,), (1,)), ((), ()))
BF16, F32 = jnp.bfloat16, jnp.float32


def scale_rows(values, norm_gain):
    mean_square = jnp.mean(values * values, axis=-1, keepdims=True)
    return values * lax.rsqrt(mean_square + EPS) * norm_gain


def norm_grad(x_float, norm_gain, grad):
    def normalize(values):
        return scale_rows(values, norm_gain)

    _, pullback = jax.vjp(normalize, x_float)
    return pullback(grad)[0].astype(BF16)


def slot_tables(index_ref, table_ref, onehot, factor, ranks, blocks, cap):
    tok = table_ref.shape[2]
    marks = jnp.concatenate(
        [jnp.where(table_ref[index_ref[b]] > 0.0, 1.0, 0.0).astype(BF16) for b in range(blocks)], axis=0
    )
    before = lax.broadcasted_iota(jnp.int32, (tok, tok), 0) < lax.broadcasted_iota(jnp.int32, (tok, tok), 1)
    ranks[...] = jnp.dot(marks, jnp.where(before, 1.0, 0.0).astype(BF16), preferred_element_type=F32)
    slots = lax.broadcasted_iota(jnp.int32, (cap, tok), 0).astype(F32)

    @pl.loop(0, blocks)
    def _(b):
        weights = table_ref[index_ref[b]]
        for e in range(2):
            weight = weights[e : e + 1, :]
            rank = jnp.where(weight > 0.0, ranks[pl.ds(2 * b + e, 1), :], -1.0)
            hit = slots == rank
            onehot[b, e * cap : (e + 1) * cap, :] = jnp.where(hit, 1.0, 0.0).astype(BF16)
            slot_weight = jnp.sum(jnp.where(hit, weight, 0.0), axis=1, keepdims=True)
            factor[e, pl.ds(pl.multiple_of(b * cap, 16), cap), :] = jnp.broadcast_to(slot_weight, (cap, tok))


def pick_rows(buffer, onehot, rows, blocks, cap):
    tok = onehot.shape[2]
    for b in blocks:
        picked = jnp.dot(onehot[b], buffer[b * tok : (b + 1) * tok, :], preferred_element_type=F32).astype(BF16)
        rows[0, b * cap : (b + 1) * cap, :] = picked[:cap]
        rows[1, b * cap : (b + 1) * cap, :] = picked[cap:]


def put_rows(buffer, onehot, rows, blocks, cap):
    tok = onehot.shape[2]
    for b in blocks:
        pair = jnp.concatenate([rows[0, b * cap : (b + 1) * cap, :], rows[1, b * cap : (b + 1) * cap, :]], axis=0)
        summed = lax.dot_general(onehot[b], pair, (((0,), (0,)), ((), ())), preferred_element_type=F32)
        buffer[b * tok : (b + 1) * tok, :] = summed.astype(BF16)


def tiles(size, most):
    step = most if size % most == 0 else size
    return [slice(at, at + step) for at in range(0, size, step)]


def forward_expert(e, rows, factor, gate_w, up_w, down_w, arrived, acts, keep, hidden):
    arrived(0), arrived(1)
    for n in tiles(gate_w.shape[1], 256):
        gate_act = jnp.dot(rows[e], gate_w[:, n], preferred_element_type=F32)
        upward = jnp.dot(rows[e], up_w[:, n], preferred_element_type=F32)
        sigmoid = jax.nn.sigmoid(gate_act)
        silu = gate_act * sigmoid
        acts[0, :, n] = (upward * sigmoid * (1.0 + gate_act * (1.0 - sigmoid))).astype(BF16)
        acts[1, :, n] = silu.astype(BF16)
        hidden[0, :, n] = (silu * upward).astype(BF16)
    keep.start()
    arrived(2)
    for n in tiles(down_w.shape[1], 512):
        total = jnp.dot(hidden[0], down_w[:, n], preferred_element_type=F32)
        rows[e, :, n] = (total * factor[e, :, :1]).astype(BF16)


def backward_expert(e, rows, factor, gate_w, up_w, down_w, arrived, acts, keep, hidden):
    arrived(2), keep.wait()
    for n in tiles(gate_w.shape[1], 256):
        grad_hidden = lax.dot_general(rows[e], down_w[n, :], PAIRS, preferred_element_type=F32)
        hidden[0, :, n] = (grad_hidden * acts[0, :, n].astype(F32)).astype(BF16)
        hidden[1, :, n] = (grad_hidden * acts[1, :, n].astype(F32)).astype(BF16)
    arrived(0), arrived(1)
    for n in tiles(down_w.shape[1], 512):
        total = lax.dot_general(hidden[0], gate_w[n, :], PAIRS, preferred_element_type=F32)
        total = total + lax.dot_general(hidden[1], up_w[n, :], PAIRS, preferred_element_type=F32)
        rows[e, :, n] = (total * factor[e, :, :1]).astype(BF16)


def experts_kernel(forward, cap, groups, index_ref, *refs):
    count = len(groups)
    table_ref, ins, weights = refs[0], refs[1 : 1 + count], refs[1 + count : 7 + count]
    rest = refs[7 + count :]
    if forward:
        outs, kept, scratch = rest[:count], rest[count], rest[count + 1 :]
    else:
        kept, outs, scratch = rest[0], rest[1 : 1 + count], rest[1 + count :]
    buffer, rows, onehot, factor, ranks, gates, ups, downs, acts, hidden, in_sem, weight_sem, act_sem = scratch
    tok = onehot.shape[2]
    blocks = sum(len(g) for g in groups)
    held = (gates, ups, downs)

    def window(i):
        return buffer.at[groups[i][0] * tok : (groups[i][-1] + 1) * tok]

    def weight_copy(e, i, source=None):
        slot = held[i].at[e]
        return pltpu.make_async_copy(slot if source is None else source, slot, weight_sem.at[3 * e + i])

    def act_copy(e):
        ends = (acts.at[e], kept.at[e]) if forward else (kept.at[e], acts.at[e])
        return pltpu.make_async_copy(*ends, act_sem.at[e])

    copies_in = [pltpu.make_async_copy(ins[i], window(i), in_sem.at[i]) for i in range(count)]
    for copy in copies_in:
        copy.start()
    for e in range(2):
        for i in (0, 1, 2) if forward else (2, 0, 1):
            weight_copy(e, i, weights[3 * e + i]).start()
        if not forward:
            act_copy(e).start()
    slot_tables(index_ref, table_ref, onehot, factor, ranks, blocks, cap)
    for copy, group in zip(copies_in, groups):
        copy.wait()
        pick_rows(buffer, onehot, rows, group, cap)

    @pl.loop(0, 2)
    def _(e):
        (forward_expert if forward else backward_expert)(
            e, rows, factor, gates.at[e], ups.at[e], downs.at[e],
            lambda i: weight_copy(e, i).wait(), acts.at[e], act_copy(e), hidden,
        )

    copies_out = [pltpu.make_async_copy(window(i), outs[i], in_sem.at[i]) for i in range(count)]
    for copy, group in zip(copies_out, groups):
        put_rows(buffer, onehot, rows, group, cap)
        copy.start()
    for copy in copies_out:
        copy.wait()
    if forward:
        for e in range(2):
            act_copy(e).wait()


def run_experts(forward, index, table, ins, weights, acts, cap):
    width, ff, tok = ins[0].shape[1], weights[0].shape[1], table.shape[2]
    groups, blocks = [], 0
    for value in ins:
        groups.append(list(range(blocks, blocks + value.shape[0] // tok)))
        blocks += value.shape[0] // tok
    slots = blocks * cap
    kept = jax.ShapeDtypeStruct((2, 2, slots, ff), BF16)
    out_shape = [jax.ShapeDtypeStruct(value.shape, BF16) for value in ins] + ([kept] if forward else [])
    in_place = pl.BlockSpec(memory_space=pl.ANY)
    operands = [index, table, *ins, *weights] + ([] if forward else [acts])
    return pl.pallas_call(
        functools.partial(experts_kernel, forward, cap, groups),
        out_shape=out_shape,
        in_specs=[pl.BlockSpec(memory_space=pltpu.SMEM), pl.BlockSpec(memory_space=pltpu.VMEM)]
        + [in_place] * (len(operands) - 2),
        out_specs=[in_place] * len(out_shape),
        scratch_shapes=[
            pltpu.VMEM((blocks * tok, width), BF16),
            pltpu.VMEM((2, slots, width), BF16),
            pltpu.VMEM((blocks, 2 * cap, tok), BF16),
            pltpu.VMEM((2, slots, tok), F32),
            pltpu.VMEM((2 * blocks, tok), F32),
            pltpu.VMEM((2, width, ff), BF16),
            pltpu.VMEM((2, width, ff), BF16),
            pltpu.VMEM((2, ff, width), BF16),
            pltpu.VMEM((2, 2, slots, ff), BF16),
            pltpu.VMEM((1 if forward else 2, slots, ff), BF16),
            pltpu.SemaphoreType.DMA((len(ins),)),
            pltpu.SemaphoreType.DMA((6,)),
            pltpu.SemaphoreType.DMA((2,)),
        ],
        compiler_params=pltpu.CompilerParams(vmem_limit_bytes=58 << 20),
        cost_estimate=pl.CostEstimate(
            flops=2 * 2 * 3 * slots * width * ff,
            bytes_accessed=2 * (6 * width * ff + 2 * blocks * tok * width) + 8 * slots * ff,
            transcendentals=2 * slots * ff,
        ),
    )(*operands)


def ep_permute(value, partner):
    return lax.ppermute(value, "ep", [(i, partner(i)) for i in range(8)])


def first(value):
    return ep_permute(value, lambda i: i ^ (4 if i & 1 else 2))


def second(value):
    return ep_permute(value, lambda i: i ^ (2 if i & 1 else 4))


def along_z(value, k):
    return lax.ppermute(value, "seq", [(i, i ^ k) for i in range(4)])


def add(*values):
    total = values[0].astype(F32)
    for value in values[1:]:
        total = total + value.astype(F32)
    return total


ORDER = (
    ("g0a", ()), ("x0a", ()), ("x2z", ()), ("x1z", ()), ("w0", ()), ("x0b", ("g0a",)), ("g0b", ("w0", "x0a",)),
    ("w2", ("w0", "x0a", "g0a",)), ("w1", ("w2",)), ("x3z", ("w2",)), ("x1a", ("x2z", "w2",)),
    ("x2a", ("w1", "x1z",)), ("x1b", ("w1", "x1z", "x2z",)), ("g2z", ("x3z", "x0b", "w1", "x1z",)),
    ("tab", ("g0b", "x3z", "x0b", "w1", "x1z",)), ("x3a", ("x1a", "g0b", "x0b", "w1",)),
    ("x2b", ("x1a", "g0b", "x3z", "x0b",)), ("x3b", ("x2a",)), ("g2a", ("x3a", "x2a",)),
    ("g3z", ("x3a", "x2a",)), ("g1z", ("x1b", "x2b", "g2z", "x3a",)), ("g2b", ("x1b", "x2b",)),
    ("F", ("g2a",)), ("o1a", ("g1z", "g2b", "g3z",)), ("g3a", ("F", "g1z", "g2b",)),
    ("o3b", ("g1z", "g2b", "g3z",)), ("g1b", ("F", "g1z", "g2b", "g3z",)), ("o1z", ()), ("g3b", ("o1a",)),
    ("o3a", ("g3a", "o1a",)), ("g1a", ("o3b", "g3a", "o1a",)), ("o2b", ("o1z", "o3b", "g3a",)),
    ("o1b", ("g1b", "o1z", "o3b", "g3a",)), ("o3z", ("g3b", "g1b", "o1z",)), ("B", ("o3a", "o1z",)),
    ("o2a", ("B", "o1b", "o3z",)), ("d3b", ("o1b", "o3z", "o2b",)), ("d2b", ("o1b", "o3z", "o2b",)),
    ("d1b", ("o1b", "o3z", "o2b",)), ("o2z", ()), ("d3a", ("o2a",)), ("d1a", ("d2b", "d3b", "o2a",)),
    ("d2a", ("d3a", "o2z",)), ("d3z", ("o2z", "d2b",)), ("d0b", ("d1a", "d3a", "o2z",)),
    ("o0b", ("d1b", "d1a", "d3a", "o2z",)), ("d2z", ("d1b", "d1a",)), ("d1z", ("d3z", "d2a", "d1b",)),
    ("d0a", ("d3z", "d2a",)), ("o0a", ("d0b", "d3z", "d2a",)),
)


def gathered(tokens, expert_ids, route_weights, norm_gain, gate_proj, up_proj, down_proj, out_grad):
    experts = lax.axis_size("seq") * lax.axis_size("ep")
    tok, fanout = expert_ids.shape
    cap = max(2, 3 * tok * fanout // (2 * experts))
    mine = (gate_proj[0], up_proj[0], down_proj[0])
    ids = jnp.arange(experts, dtype=jnp.int32)
    routes = jnp.sum(
        jnp.where(expert_ids[:, :, None] == ids[None, None, :], route_weights[:, :, None], 0.0), axis=1
    )
    pairs = routes.T.reshape(experts // 2, 2, tok)
    for_device = jnp.stack([pairs, pairs[:, ::-1]], axis=1).reshape(experts, 2 * tok)
    x_float = tokens.astype(F32)
    normed = scale_rows(x_float, norm_gain).astype(BF16)
    z, ep = lax.axis_index("seq"), lax.axis_index("ep")
    core = ep % 2
    step_first = jnp.where(core == 1, 4, 2)
    step_second = jnp.where(core == 1, 2, 4)
    masks = [0, step_first, step_second, step_first | step_second]
    done = {"x0": normed, "g0": out_grad}

    def experts_pass(forward, offsets, source, target, acts, wait):
        keys = [(k, s) for k in offsets for s in "0ab"]
        blocks = [(k, j) for k, s in keys for j in ((2, 3) if s == "b" else ("0a".index(s),))]
        index = jnp.stack([(z ^ k) * 8 + (ep ^ masks[j]) for k, j in blocks]).astype(jnp.int32)
        arrays = [done[source + ("0" if (k, s) == (0, "0") else f"{k}z" if s == "0" else f"{k}{s}")] for k, s in keys]
        theirs = tuple(done[f"w{i}"] for i in range(3))
        table = done["tab"].reshape(experts, 2, tok)
        out = run_experts(forward, wait(index), table, arrays, mine + theirs, acts, cap)
        for (k, s), value in zip(keys, out):
            done[f"{target}part{k}{s}"] = value
        return out

    def spread_step(name, wait):
        t, k, move = name[0], int(name[1]), name[2]
        own = done[f"{t}0"]
        if move == "z":
            return along_z(wait(done[f"{t}2z"]), 1) if k == 3 else along_z(wait(own), k)
        if name[1:] == "1b":
            return along_z(wait(done[f"{t}0b"]), 1)
        shard = own if k == 0 else done[f"{t}{k}z"]
        if move == "a":
            return first(wait(shard))
        return second(jnp.concatenate([shard, wait(done[f"{t}{k}a"])], axis=0))

    def merge_step(name, wait):
        t, k, move = name[0], int(name[1]), name[2]

        def part(s):
            return done[f"{t}part{k}{s}"]

        if name[1:] == "1b":
            return along_z(wait(part("b")), 1)
        if move == "b":
            value = add(part("b"), done[f"{t}1b"]).astype(BF16) if k == 0 else part("b")
            return second(wait(value))
        if move == "a":
            value = part("a") if k == 1 else add(part("a"), done[f"{t}{k}b"][tok:]).astype(BF16)
            return first(wait(value))
        value = total(t, k)
        return along_z(wait(value.astype(BF16)), 2 if k == 2 else 1)

    def total(t, k):
        values = [done[f"{t}part{k}0"], done[f"{t}{k}a"]]
        if k != 1:
            values.append(done[f"{t}{k}b"][:tok])
        if k == 2:
            values.append(done[f"{t}3z"])
        if k == 0:
            values += [done[f"{t}1z"], done[f"{t}2z"]]
        return add(*values)

    acts = {}
    for name, others in ORDER:

        def wait(value, others=others):
            if not others:
                return value
            return lax.optimization_barrier((value, *[done[n] for n in others]))[0]

        with jax.named_scope(name):
            if name[0] in "FB":
                offsets = {"0": (0, 2), "1": (1, 3)}.get(name[1:], (0, 1, 2, 3))
                if name[0] == "F":
                    out = experts_pass(True, offsets, "x", "o", None, wait)
                    acts[offsets] = out[-1]
                else:
                    out = experts_pass(False, offsets, "g", "d", acts[offsets], wait)
                done[name] = out[0]
            elif name == "tab":
                done[name] = lax.all_to_all(wait(for_device), ("seq", "ep"), split_axis=0, concat_axis=0, tiled=True)
            elif name[0] == "w":
                done[name] = ep_permute(wait(mine[int(name[1])]), lambda i: i ^ 1)
            else:
                done[name] = (spread_step if name[0] in "xg" else merge_step)(name, wait)
    return (total("o", 0).astype(BF16), norm_grad(x_float, norm_gain, total("d", 0)))


def expert_forward(inputs, gate_w, up_w, down_w):
    gate_act = jnp.dot(inputs, gate_w, preferred_element_type=jnp.float32)
    upward = jnp.dot(inputs, up_w, preferred_element_type=jnp.float32)
    hidden = (jax.nn.silu(gate_act) * upward).astype(jnp.bfloat16)
    result = jnp.dot(hidden, down_w, preferred_element_type=jnp.float32).astype(jnp.bfloat16)
    return (result, gate_act, upward)


def expert_backward(grads, gate_act, upward, gate_w, up_w, down_w):
    pairs = (((1,), (1,)), ((), ()))
    grad_hidden = lax.dot_general(grads, down_w, pairs, preferred_element_type=jnp.float32)
    sigmoid_gate = jax.nn.sigmoid(gate_act)
    grad_gate = (
        grad_hidden * upward * sigmoid_gate * (1.0 + gate_act * (1.0 - sigmoid_gate))
    ).astype(jnp.bfloat16)
    grad_up = (grad_hidden * (gate_act * sigmoid_gate)).astype(jnp.bfloat16)
    summed = lax.dot_general(grad_gate, gate_w, pairs, preferred_element_type=jnp.float32)
    summed = summed + lax.dot_general(grad_up, up_w, pairs, preferred_element_type=jnp.float32)
    return summed.astype(jnp.bfloat16)


def move_out(slots):
    arrived = lax.all_to_all(slots, ("seq", "ep"), split_axis=0, concat_axis=0, tiled=True)
    return arrived


def move_back(slots):
    arrived = lax.all_to_all(slots, ("seq", "ep"), split_axis=0, concat_axis=0, tiled=True)
    return arrived


def run_live(compute, inputs):
    outputs = list(compute(inputs))
    return outputs


def exchanged(tokens, expert_ids, route_weights, norm_gain, gate_proj, up_proj, down_proj, out_grad):
    own_weights = (gate_proj[0], up_proj[0], down_proj[0])
    experts = lax.axis_size("seq") * lax.axis_size("ep")
    tok_count, fanout = expert_ids.shape
    model_width = tokens.shape[1]
    capacity = max(2, 3 * tok_count * fanout // (2 * experts))
    zero_value = jnp.zeros((), jnp.bfloat16)
    x_float = tokens.astype(jnp.float32)
    normed = scale_rows(x_float, norm_gain).astype(jnp.bfloat16)
    flat_ids = expert_ids.reshape(-1)
    one_hot = (flat_ids[:, None] == jnp.arange(experts, dtype=jnp.int32)[None, :]).astype(jnp.int32)
    slot_rank = jnp.sum((jnp.cumsum(one_hot, axis=0) - one_hot) * one_hot, axis=1)
    groups = [(0, capacity, own_weights)]
    position = flat_ids * capacity + slot_rank
    slot_route = (
        jnp.full((experts * capacity,), -1, jnp.int32)
        .at[position]
        .set(jnp.arange(flat_ids.shape[0], dtype=jnp.int32))
    )
    alive_slot = slot_route >= 0
    source = jnp.maximum(slot_route, 0) // fanout
    outgoing = jnp.where(alive_slot[:, None], normed[source], zero_value).reshape(
        experts, capacity, model_width
    )
    arrived = move_out(outgoing)
    first, width, weight_set = groups[0]
    inputs = arrived.reshape(-1, model_width)
    alive_rows = jnp.any(inputs != 0, axis=1)

    def forward_pass(parts, weight_set=weight_set):
        return expert_forward(parts[0], *weight_set)

    result, gate_act, upward = run_live(forward_pass, [inputs])
    saved = [(gate_act, upward, alive_rows)]
    result_parts = result.reshape(experts, width, model_width)
    route_out = move_back(result_parts).reshape(-1, model_width)[position]
    outgoing_grad = jnp.where(alive_slot[:, None], out_grad[source], zero_value).reshape(
        experts, capacity, model_width
    )
    grads_arrived = move_out(outgoing_grad)
    grad_parts = []
    for (first, width, weight_set), (gate_act, upward, alive_rows) in zip(groups, saved):
        grads = grads_arrived.reshape(-1, model_width)

        def backward_pass(parts, weight_set=weight_set):
            return (expert_backward(parts[0], parts[1], parts[2], *weight_set),)

        grad_rows = run_live(backward_pass, [grads, gate_act, upward])[0]
        grad_parts.append(grad_rows.reshape(experts, width, model_width))
    route_grad = move_back(grad_parts[0]).reshape(-1, model_width)[position]
    weight_cube = route_weights[:, :, None]
    moe_out = jnp.sum(
        weight_cube * route_out.reshape(tok_count, fanout, model_width).astype(jnp.float32), axis=1
    ).astype(jnp.bfloat16)
    grad_normed = jnp.sum(
        weight_cube * route_grad.reshape(tok_count, fanout, model_width).astype(jnp.float32), axis=1
    )

    def normalize(values):
        return scale_rows(values, norm_gain)

    _, pullback = jax.vjp(normalize, x_float)
    in_grad = pullback(grad_normed)[0].astype(jnp.bfloat16)
    return (moe_out, in_grad)


def solution(mesh):
    rows = P(("seq", "ep"), None)
    cubes = P(("seq", "ep"), None, None)
    planes = mesh.shape["seq"] == 4 and mesh.shape["ep"] == 8
    return jax.shard_map(
        gathered if planes else exchanged,
        mesh=mesh,
        in_specs=(rows, rows, rows, P(), cubes, cubes, cubes, rows),
        out_specs=(rows, rows),
        check_vma=False,
    )
```

```python
import functools

import jax
import jax.numpy as jnp
from jax import lax
from jax.experimental import pallas as pl
from jax.experimental.pallas import tpu as pltpu
from jax.sharding import PartitionSpec as P

EPS = 1e-06
PAIRS = (((1,), (1,)), ((), ()))
BF16, F32 = jnp.bfloat16, jnp.float32


def scale_rows(values, norm_gain):
    mean_square = jnp.mean(values * values, axis=-1, keepdims=True)
    return values * lax.rsqrt(mean_square + EPS) * norm_gain


def norm_grad(x_float, norm_gain, grad):
    def normalize(values):
        return scale_rows(values, norm_gain)

    _, pullback = jax.vjp(normalize, x_float)
    return pullback(grad)[0].astype(BF16)


def slot_tables(index_ref, table_ref, onehot, factor, ranks, blocks, cap):
    tok = table_ref.shape[2]
    marks = jnp.concatenate(
        [jnp.where(table_ref[index_ref[b]] > 0.0, 1.0, 0.0).astype(BF16) for b in range(blocks)], axis=0
    )
    before = lax.broadcasted_iota(jnp.int32, (tok, tok), 0) < lax.broadcasted_iota(jnp.int32, (tok, tok), 1)
    ranks[...] = jnp.dot(marks, jnp.where(before, 1.0, 0.0).astype(BF16), preferred_element_type=F32)
    slots = lax.broadcasted_iota(jnp.int32, (cap, tok), 0).astype(F32)

    @pl.loop(0, blocks)
    def _(b):
        weights = table_ref[index_ref[b]]
        for e in range(2):
            weight = weights[e : e + 1, :]
            rank = jnp.where(weight > 0.0, ranks[pl.ds(2 * b + e, 1), :], -1.0)
            hit = slots == rank
            onehot[b, e * cap : (e + 1) * cap, :] = jnp.where(hit, 1.0, 0.0).astype(BF16)
            slot_weight = jnp.sum(jnp.where(hit, weight, 0.0), axis=1, keepdims=True)
            factor[e, pl.ds(pl.multiple_of(b * cap, 16), cap), :] = jnp.broadcast_to(slot_weight, (cap, tok))


def pick_rows(buffer, onehot, rows, blocks, cap):
    tok = onehot.shape[2]
    for b in blocks:
        picked = jnp.dot(onehot[b], buffer[b * tok : (b + 1) * tok, :], preferred_element_type=F32).astype(BF16)
        rows[0, b * cap : (b + 1) * cap, :] = picked[:cap]
        rows[1, b * cap : (b + 1) * cap, :] = picked[cap:]


def put_rows(buffer, onehot, rows, blocks, cap):
    tok = onehot.shape[2]
    for b in blocks:
        pair = jnp.concatenate([rows[0, b * cap : (b + 1) * cap, :], rows[1, b * cap : (b + 1) * cap, :]], axis=0)
        summed = lax.dot_general(onehot[b], pair, (((0,), (0,)), ((), ())), preferred_element_type=F32)
        buffer[b * tok : (b + 1) * tok, :] = summed.astype(BF16)


def tiles(size, most):
    step = most if size % most == 0 else size
    return [slice(at, at + step) for at in range(0, size, step)]


def forward_expert(e, rows, factor, gate_w, up_w, down_w, arrived, acts, keep, hidden):
    arrived(0), arrived(1)
    for n in tiles(gate_w.shape[1], 256):
        gate_act = jnp.dot(rows[e], gate_w[:, n], preferred_element_type=F32)
        upward = jnp.dot(rows[e], up_w[:, n], preferred_element_type=F32)
        sigmoid = jax.nn.sigmoid(gate_act)
        silu = gate_act * sigmoid
        acts[0, :, n] = (upward * sigmoid * (1.0 + gate_act * (1.0 - sigmoid))).astype(BF16)
        acts[1, :, n] = silu.astype(BF16)
        hidden[0, :, n] = (silu * upward).astype(BF16)
    keep.start()
    arrived(2)
    for n in tiles(down_w.shape[1], 512):
        total = jnp.dot(hidden[0], down_w[:, n], preferred_element_type=F32)
        rows[e, :, n] = (total * factor[e, :, :1]).astype(BF16)


def backward_expert(e, rows, factor, gate_w, up_w, down_w, arrived, acts, keep, hidden):
    arrived(2), keep.wait()
    for n in tiles(gate_w.shape[1], 256):
        grad_hidden = lax.dot_general(rows[e], down_w[n, :], PAIRS, preferred_element_type=F32)
        hidden[0, :, n] = (grad_hidden * acts[0, :, n].astype(F32)).astype(BF16)
        hidden[1, :, n] = (grad_hidden * acts[1, :, n].astype(F32)).astype(BF16)
    arrived(0), arrived(1)
    for n in tiles(down_w.shape[1], 512):
        total = lax.dot_general(hidden[0], gate_w[n, :], PAIRS, preferred_element_type=F32)
        total = total + lax.dot_general(hidden[1], up_w[n, :], PAIRS, preferred_element_type=F32)
        rows[e, :, n] = (total * factor[e, :, :1]).astype(BF16)


def experts_kernel(forward, cap, groups, index_ref, *refs):
    count = len(groups)
    table_ref, ins, weights = refs[0], refs[1 : 1 + count], refs[1 + count : 7 + count]
    rest = refs[7 + count :]
    if forward:
        outs, kept, scratch = rest[:count], rest[count], rest[count + 1 :]
    else:
        kept, outs, scratch = rest[0], rest[1 : 1 + count], rest[1 + count :]
    buffer, rows, onehot, factor, ranks, gates, ups, downs, acts, hidden, in_sem, weight_sem, act_sem = scratch
    tok = onehot.shape[2]
    blocks = sum(len(g) for g in groups)
    held = (gates, ups, downs)

    def window(i):
        return buffer.at[groups[i][0] * tok : (groups[i][-1] + 1) * tok]

    def weight_copy(e, i, source=None):
        slot = held[i].at[e]
        return pltpu.make_async_copy(slot if source is None else source, slot, weight_sem.at[3 * e + i])

    def act_copy(e):
        ends = (acts.at[e], kept.at[e]) if forward else (kept.at[e], acts.at[e])
        return pltpu.make_async_copy(*ends, act_sem.at[e])

    copies_in = [pltpu.make_async_copy(ins[i], window(i), in_sem.at[i]) for i in range(count)]
    for copy in copies_in:
        copy.start()
    for e in range(2):
        for i in (0, 1, 2) if forward else (2, 0, 1):
            weight_copy(e, i, weights[3 * e + i]).start()
        if not forward:
            act_copy(e).start()
    slot_tables(index_ref, table_ref, onehot, factor, ranks, blocks, cap)
    for copy, group in zip(copies_in, groups):
        copy.wait()
        pick_rows(buffer, onehot, rows, group, cap)

    @pl.loop(0, 2)
    def _(e):
        (forward_expert if forward else backward_expert)(
            e, rows, factor, gates.at[e], ups.at[e], downs.at[e],
            lambda i: weight_copy(e, i).wait(), acts.at[e], act_copy(e), hidden,
        )

    copies_out = [pltpu.make_async_copy(window(i), outs[i], in_sem.at[i]) for i in range(count)]
    for copy, group in zip(copies_out, groups):
        put_rows(buffer, onehot, rows, group, cap)
        copy.start()
    for copy in copies_out:
        copy.wait()
    if forward:
        for e in range(2):
            act_copy(e).wait()


def run_experts(forward, index, table, ins, weights, acts, cap):
    width, ff, tok = ins[0].shape[1], weights[0].shape[1], table.shape[2]
    groups, blocks = [], 0
    for value in ins:
        groups.append(list(range(blocks, blocks + value.shape[0] // tok)))
        blocks += value.shape[0] // tok
    slots = blocks * cap
    kept = jax.ShapeDtypeStruct((2, 2, slots, ff), BF16)
    out_shape = [jax.ShapeDtypeStruct(value.shape, BF16) for value in ins] + ([kept] if forward else [])
    in_place = pl.BlockSpec(memory_space=pl.ANY)
    operands = [index, table, *ins, *weights] + ([] if forward else [acts])
    return pl.pallas_call(
        functools.partial(experts_kernel, forward, cap, groups),
        out_shape=out_shape,
        in_specs=[pl.BlockSpec(memory_space=pltpu.SMEM), pl.BlockSpec(memory_space=pltpu.VMEM)]
        + [in_place] * (len(operands) - 2),
        out_specs=[in_place] * len(out_shape),
        scratch_shapes=[
            pltpu.VMEM((blocks * tok, width), BF16),
            pltpu.VMEM((2, slots, width), BF16),
            pltpu.VMEM((blocks, 2 * cap, tok), BF16),
            pltpu.VMEM((2, slots, tok), F32),
            pltpu.VMEM((2 * blocks, tok), F32),
            pltpu.VMEM((2, width, ff), BF16),
            pltpu.VMEM((2, width, ff), BF16),
            pltpu.VMEM((2, ff, width), BF16),
            pltpu.VMEM((2, 2, slots, ff), BF16),
            pltpu.VMEM((1 if forward else 2, slots, ff), BF16),
            pltpu.SemaphoreType.DMA((len(ins),)),
            pltpu.SemaphoreType.DMA((6,)),
            pltpu.SemaphoreType.DMA((2,)),
        ],
        compiler_params=pltpu.CompilerParams(vmem_limit_bytes=58 << 20),
        cost_estimate=pl.CostEstimate(
            flops=2 * 2 * 3 * slots * width * ff,
            bytes_accessed=2 * (6 * width * ff + 2 * blocks * tok * width) + 8 * slots * ff,
            transcendentals=2 * slots * ff,
        ),
    )(*operands)


def ep_permute(value, partner):
    return lax.ppermute(value, "ep", [(i, partner(i)) for i in range(8)])


def first(value):
    return ep_permute(value, lambda i: i ^ (4 if i & 1 else 2))


def second(value):
    return ep_permute(value, lambda i: i ^ (2 if i & 1 else 4))


def along_z(value, k):
    return lax.ppermute(value, "seq", [(i, i ^ k) for i in range(4)])


def add(*values):
    total = values[0].astype(F32)
    for value in values[1:]:
        total = total + value.astype(F32)
    return total


ORDER = (
    ("g0a", ()), ("x0a", ()), ("x2z", ()), ("x1z", ()), ("w0", ()), ("x0b", ("g0a",)), ("g0b", ("w0", "x0a",)),
    ("w2", ("w0", "x0a", "g0a",)), ("w1", ("w2",)), ("x3z", ("w2",)), ("x1a", ("x2z", "w2",)),
    ("x2a", ("w1", "x1z",)), ("x1b", ("w1", "x1z", "x2z",)), ("g2z", ("x3z", "x0b", "w1", "x1z",)),
    ("tab", ("g0b", "x3z", "x0b", "w1", "x1z",)), ("x3a", ("x1a", "g0b", "x0b", "w1",)),
    ("x2b", ("x1a", "g0b", "x3z", "x0b",)), ("x3b", ("x2a",)), ("g2a", ("x3a", "x2a",)),
    ("g3z", ("x3a", "x2a",)), ("g1z", ("x1b", "x2b", "g2z", "x3a",)), ("g2b", ("x1b", "x2b",)),
    ("F", ("g2a",)), ("o1a", ("g1z", "g2b", "g3z",)), ("g3a", ("F", "g1z", "g2b",)),
    ("o3b", ("g1z", "g2b", "g3z",)), ("g1b", ("F", "g1z", "g2b", "g3z",)), ("o1z", ()), ("g3b", ("o1a",)),
    ("o3a", ("g3a", "o1a",)), ("g1a", ("o3b", "g3a", "o1a",)), ("o2b", ("o1z", "o3b", "g3a",)),
    ("o1b", ("g1b", "o1z", "o3b", "g3a",)), ("o3z", ("g3b", "g1b", "o1z",)), ("B", ("o3a", "o1z",)),
    ("o2a", ("B",)), ("d3b", ()), ("d2b", ()), ("d1b", ()), ("o2z", ()), ("d3a", ()), ("d1a", ()), ("d2a", ()),
    ("d3z", ()), ("d0b", ()), ("o0b", ()), ("d2z", ()), ("d1z", ()), ("d0a", ()), ("o0a", ()),
)


def gathered(tokens, expert_ids, route_weights, norm_gain, gate_proj, up_proj, down_proj, out_grad):
    experts = lax.axis_size("seq") * lax.axis_size("ep")
    tok, fanout = expert_ids.shape
    cap = max(2, 3 * tok * fanout // (2 * experts))
    mine = (gate_proj[0], up_proj[0], down_proj[0])
    ids = jnp.arange(experts, dtype=jnp.int32)
    routes = jnp.sum(
        jnp.where(expert_ids[:, :, None] == ids[None, None, :], route_weights[:, :, None], 0.0), axis=1
    )
    pairs = routes.T.reshape(experts // 2, 2, tok)
    for_device = jnp.stack([pairs, pairs[:, ::-1]], axis=1).reshape(experts, 2 * tok)
    x_float = tokens.astype(F32)
    normed = scale_rows(x_float, norm_gain).astype(BF16)
    z, ep = lax.axis_index("seq"), lax.axis_index("ep")
    core = ep % 2
    step_first = jnp.where(core == 1, 4, 2)
    step_second = jnp.where(core == 1, 2, 4)
    masks = [0, step_first, step_second, step_first | step_second]
    done = {"x0": normed, "g0": out_grad}

    def experts_pass(forward, offsets, source, target, acts, wait):
        keys = [(k, s) for k in offsets for s in "0ab"]
        blocks = [(k, j) for k, s in keys for j in ((2, 3) if s == "b" else ("0a".index(s),))]
        index = jnp.stack([(z ^ k) * 8 + (ep ^ masks[j]) for k, j in blocks]).astype(jnp.int32)
        arrays = [done[source + ("0" if (k, s) == (0, "0") else f"{k}z" if s == "0" else f"{k}{s}")] for k, s in keys]
        theirs = tuple(done[f"w{i}"] for i in range(3))
        table = done["tab"].reshape(experts, 2, tok)
        out = run_experts(forward, wait(index), table, arrays, mine + theirs, acts, cap)
        for (k, s), value in zip(keys, out):
            done[f"{target}part{k}{s}"] = value
        return out

    def spread_step(name, wait):
        t, k, move = name[0], int(name[1]), name[2]
        own = done[f"{t}0"]
        if move == "z":
            return along_z(wait(done[f"{t}2z"]), 1) if k == 3 else along_z(wait(own), k)
        if name[1:] == "1b":
            return along_z(wait(done[f"{t}0b"]), 1)
        shard = own if k == 0 else done[f"{t}{k}z"]
        if move == "a":
            return first(wait(shard))
        return second(jnp.concatenate([shard, wait(done[f"{t}{k}a"])], axis=0))

    def merge_step(name, wait):
        t, k, move = name[0], int(name[1]), name[2]

        def part(s):
            return done[f"{t}part{k}{s}"]

        if name[1:] == "1b":
            return along_z(wait(part("b")), 1)
        if move == "b":
            value = add(part("b"), done[f"{t}1b"]).astype(BF16) if k == 0 else part("b")
            return second(wait(value))
        if move == "a":
            value = part("a") if k == 1 else add(part("a"), done[f"{t}{k}b"][tok:]).astype(BF16)
            return first(wait(value))
        value = total(t, k)
        return along_z(wait(value.astype(BF16)), 2 if k == 2 else 1)

    def total(t, k):
        values = [done[f"{t}part{k}0"], done[f"{t}{k}a"]]
        if k != 1:
            values.append(done[f"{t}{k}b"][:tok])
        if k == 2:
            values.append(done[f"{t}3z"])
        if k == 0:
            values += [done[f"{t}1z"], done[f"{t}2z"]]
        return add(*values)

    acts = {}
    for name, others in ORDER:

        def wait(value, others=others):
            if not others:
                return value
            return lax.optimization_barrier((value, *[done[n] for n in others]))[0]

        with jax.named_scope(name):
            if name[0] in "FB":
                offsets = {"0": (0, 2), "1": (1, 3)}.get(name[1:], (0, 1, 2, 3))
                if name[0] == "F":
                    out = experts_pass(True, offsets, "x", "o", None, wait)
                    acts[offsets] = out[-1]
                else:
                    out = experts_pass(False, offsets, "g", "d", acts[offsets], wait)
                done[name] = out[0]
            elif name == "tab":
                done[name] = lax.all_to_all(wait(for_device), ("seq", "ep"), split_axis=0, concat_axis=0, tiled=True)
            elif name[0] == "w":
                done[name] = ep_permute(wait(mine[int(name[1])]), lambda i: i ^ 1)
            else:
                done[name] = (spread_step if name[0] in "xg" else merge_step)(name, wait)
    return (total("o", 0).astype(BF16), norm_grad(x_float, norm_gain, total("d", 0)))


def expert_forward(inputs, gate_w, up_w, down_w):
    gate_act = jnp.dot(inputs, gate_w, preferred_element_type=jnp.float32)
    upward = jnp.dot(inputs, up_w, preferred_element_type=jnp.float32)
    hidden = (jax.nn.silu(gate_act) * upward).astype(jnp.bfloat16)
    result = jnp.dot(hidden, down_w, preferred_element_type=jnp.float32).astype(jnp.bfloat16)
    return (result, gate_act, upward)


def expert_backward(grads, gate_act, upward, gate_w, up_w, down_w):
    pairs = (((1,), (1,)), ((), ()))
    grad_hidden = lax.dot_general(grads, down_w, pairs, preferred_element_type=jnp.float32)
    sigmoid_gate = jax.nn.sigmoid(gate_act)
    grad_gate = (
        grad_hidden * upward * sigmoid_gate * (1.0 + gate_act * (1.0 - sigmoid_gate))
    ).astype(jnp.bfloat16)
    grad_up = (grad_hidden * (gate_act * sigmoid_gate)).astype(jnp.bfloat16)
    summed = lax.dot_general(grad_gate, gate_w, pairs, preferred_element_type=jnp.float32)
    summed = summed + lax.dot_general(grad_up, up_w, pairs, preferred_element_type=jnp.float32)
    return summed.astype(jnp.bfloat16)


def move_out(slots):
    arrived = lax.all_to_all(slots, ("seq", "ep"), split_axis=0, concat_axis=0, tiled=True)
    return arrived


def move_back(slots):
    arrived = lax.all_to_all(slots, ("seq", "ep"), split_axis=0, concat_axis=0, tiled=True)
    return arrived


def run_live(compute, inputs):
    outputs = list(compute(inputs))
    return outputs


def exchanged(tokens, expert_ids, route_weights, norm_gain, gate_proj, up_proj, down_proj, out_grad):
    own_weights = (gate_proj[0], up_proj[0], down_proj[0])
    experts = lax.axis_size("seq") * lax.axis_size("ep")
    tok_count, fanout = expert_ids.shape
    model_width = tokens.shape[1]
    capacity = max(2, 3 * tok_count * fanout // (2 * experts))
    zero_value = jnp.zeros((), jnp.bfloat16)
    x_float = tokens.astype(jnp.float32)
    normed = scale_rows(x_float, norm_gain).astype(jnp.bfloat16)
    flat_ids = expert_ids.reshape(-1)
    one_hot = (flat_ids[:, None] == jnp.arange(experts, dtype=jnp.int32)[None, :]).astype(jnp.int32)
    slot_rank = jnp.sum((jnp.cumsum(one_hot, axis=0) - one_hot) * one_hot, axis=1)
    groups = [(0, capacity, own_weights)]
    position = flat_ids * capacity + slot_rank
    slot_route = (
        jnp.full((experts * capacity,), -1, jnp.int32)
        .at[position]
        .set(jnp.arange(flat_ids.shape[0], dtype=jnp.int32))
    )
    alive_slot = slot_route >= 0
    source = jnp.maximum(slot_route, 0) // fanout
    outgoing = jnp.where(alive_slot[:, None], normed[source], zero_value).reshape(
        experts, capacity, model_width
    )
    arrived = move_out(outgoing)
    first, width, weight_set = groups[0]
    inputs = arrived.reshape(-1, model_width)
    alive_rows = jnp.any(inputs != 0, axis=1)

    def forward_pass(parts, weight_set=weight_set):
        return expert_forward(parts[0], *weight_set)

    result, gate_act, upward = run_live(forward_pass, [inputs])
    saved = [(gate_act, upward, alive_rows)]
    result_parts = result.reshape(experts, width, model_width)
    route_out = move_back(result_parts).reshape(-1, model_width)[position]
    outgoing_grad = jnp.where(alive_slot[:, None], out_grad[source], zero_value).reshape(
        experts, capacity, model_width
    )
    grads_arrived = move_out(outgoing_grad)
    grad_parts = []
    for (first, width, weight_set), (gate_act, upward, alive_rows) in zip(groups, saved):
        grads = grads_arrived.reshape(-1, model_width)

        def backward_pass(parts, weight_set=weight_set):
            return (expert_backward(parts[0], parts[1], parts[2], *weight_set),)

        grad_rows = run_live(backward_pass, [grads, gate_act, upward])[0]
        grad_parts.append(grad_rows.reshape(experts, width, model_width))
    route_grad = move_back(grad_parts[0]).reshape(-1, model_width)[position]
    weight_cube = route_weights[:, :, None]
    moe_out = jnp.sum(
        weight_cube * route_out.reshape(tok_count, fanout, model_width).astype(jnp.float32), axis=1
    ).astype(jnp.bfloat16)
    grad_normed = jnp.sum(
        weight_cube * route_grad.reshape(tok_count, fanout, model_width).astype(jnp.float32), axis=1
    )

    def normalize(values):
        return scale_rows(values, norm_gain)

    _, pullback = jax.vjp(normalize, x_float)
    in_grad = pullback(grad_normed)[0].astype(jnp.bfloat16)
    return (moe_out, in_grad)


def solution(mesh):
    rows = P(("seq", "ep"), None)
    cubes = P(("seq", "ep"), None, None)
    planes = mesh.shape["seq"] == 4 and mesh.shape["ep"] == 8
    return jax.shard_map(
        gathered if planes else exchanged,
        mesh=mesh,
        in_specs=(rows, rows, rows, P(), cubes, cubes, cubes, rows),
        out_specs=(rows, rows),
        check_vma=False,
    )
```

```python
import functools

import jax
import jax.numpy as jnp
from jax import lax
from jax.experimental import pallas as pl
from jax.experimental.pallas import tpu as pltpu
from jax.sharding import PartitionSpec as P

EPS = 1e-06
PAIRS = (((1,), (1,)), ((), ()))
BF16, F32 = jnp.bfloat16, jnp.float32


def scale_rows(values, norm_gain):
    mean_square = jnp.mean(values * values, axis=-1, keepdims=True)
    return values * lax.rsqrt(mean_square + EPS) * norm_gain


def norm_grad(x_float, norm_gain, grad):
    def normalize(values):
        return scale_rows(values, norm_gain)

    _, pullback = jax.vjp(normalize, x_float)
    return pullback(grad)[0].astype(BF16)


def slot_tables(index_ref, table_ref, onehot, factor, ranks, blocks, cap):
    tok = table_ref.shape[2]
    marks = jnp.concatenate(
        [jnp.where(table_ref[index_ref[b]] > 0.0, 1.0, 0.0).astype(BF16) for b in range(blocks)], axis=0
    )
    before = lax.broadcasted_iota(jnp.int32, (tok, tok), 0) < lax.broadcasted_iota(jnp.int32, (tok, tok), 1)
    ranks[...] = jnp.dot(marks, jnp.where(before, 1.0, 0.0).astype(BF16), preferred_element_type=F32)
    slots = lax.broadcasted_iota(jnp.int32, (cap, tok), 0).astype(F32)

    @pl.loop(0, blocks)
    def _(b):
        weights = table_ref[index_ref[b]]
        for e in range(2):
            weight = weights[e : e + 1, :]
            rank = jnp.where(weight > 0.0, ranks[pl.ds(2 * b + e, 1), :], -1.0)
            hit = slots == rank
            onehot[b, e * cap : (e + 1) * cap, :] = jnp.where(hit, 1.0, 0.0).astype(BF16)
            slot_weight = jnp.sum(jnp.where(hit, weight, 0.0), axis=1, keepdims=True)
            factor[e, pl.ds(pl.multiple_of(b * cap, 16), cap), :] = jnp.broadcast_to(slot_weight, (cap, tok))


def pick_rows(buffer, onehot, rows, blocks, cap):
    tok = onehot.shape[2]
    for b in blocks:
        picked = jnp.dot(onehot[b], buffer[b * tok : (b + 1) * tok, :], preferred_element_type=F32).astype(BF16)
        rows[0, b * cap : (b + 1) * cap, :] = picked[:cap]
        rows[1, b * cap : (b + 1) * cap, :] = picked[cap:]


def put_rows(buffer, onehot, rows, blocks, cap):
    tok = onehot.shape[2]
    for b in blocks:
        pair = jnp.concatenate([rows[0, b * cap : (b + 1) * cap, :], rows[1, b * cap : (b + 1) * cap, :]], axis=0)
        summed = lax.dot_general(onehot[b], pair, (((0,), (0,)), ((), ())), preferred_element_type=F32)
        buffer[b * tok : (b + 1) * tok, :] = summed.astype(BF16)


def tiles(size, most):
    step = most if size % most == 0 else size
    return [slice(at, at + step) for at in range(0, size, step)]


def forward_expert(e, rows, factor, gate_w, up_w, down_w, arrived, acts, keep, hidden):
    arrived(0), arrived(1)
    for n in tiles(gate_w.shape[1], 256):
        gate_act = jnp.dot(rows[e], gate_w[:, n], preferred_element_type=F32)
        upward = jnp.dot(rows[e], up_w[:, n], preferred_element_type=F32)
        sigmoid = jax.nn.sigmoid(gate_act)
        silu = gate_act * sigmoid
        acts[0, :, n] = (upward * sigmoid * (1.0 + gate_act * (1.0 - sigmoid))).astype(BF16)
        acts[1, :, n] = silu.astype(BF16)
        hidden[0, :, n] = (silu * upward).astype(BF16)
    keep.start()
    arrived(2)
    for n in tiles(down_w.shape[1], 512):
        total = jnp.dot(hidden[0], down_w[:, n], preferred_element_type=F32)
        rows[e, :, n] = (total * factor[e, :, :1]).astype(BF16)


def backward_expert(e, rows, factor, gate_w, up_w, down_w, arrived, acts, keep, hidden):
    arrived(2), keep.wait()
    for n in tiles(gate_w.shape[1], 256):
        grad_hidden = lax.dot_general(rows[e], down_w[n, :], PAIRS, preferred_element_type=F32)
        hidden[0, :, n] = (grad_hidden * acts[0, :, n].astype(F32)).astype(BF16)
        hidden[1, :, n] = (grad_hidden * acts[1, :, n].astype(F32)).astype(BF16)
    arrived(0), arrived(1)
    for n in tiles(down_w.shape[1], 512):
        total = lax.dot_general(hidden[0], gate_w[n, :], PAIRS, preferred_element_type=F32)
        total = total + lax.dot_general(hidden[1], up_w[n, :], PAIRS, preferred_element_type=F32)
        rows[e, :, n] = (total * factor[e, :, :1]).astype(BF16)


def experts_kernel(forward, cap, groups, index_ref, *refs):
    count = len(groups)
    table_ref, ins, weights = refs[0], refs[1 : 1 + count], refs[1 + count : 7 + count]
    rest = refs[7 + count :]
    if forward:
        outs, kept, scratch = rest[:count], rest[count], rest[count + 1 :]
    else:
        kept, outs, scratch = rest[0], rest[1 : 1 + count], rest[1 + count :]
    buffer, rows, onehot, factor, ranks, gates, ups, downs, acts, hidden, in_sem, weight_sem, act_sem = scratch
    tok = onehot.shape[2]
    blocks = sum(len(g) for g in groups)
    held = (gates, ups, downs)

    def window(i):
        return buffer.at[groups[i][0] * tok : (groups[i][-1] + 1) * tok]

    def weight_copy(e, i, source=None):
        slot = held[i].at[e]
        return pltpu.make_async_copy(slot if source is None else source, slot, weight_sem.at[3 * e + i])

    def act_copy(e):
        ends = (acts.at[e], kept.at[e]) if forward else (kept.at[e], acts.at[e])
        return pltpu.make_async_copy(*ends, act_sem.at[e])

    copies_in = [pltpu.make_async_copy(ins[i], window(i), in_sem.at[i]) for i in range(count)]
    for copy in copies_in:
        copy.start()
    for e in range(2):
        for i in (0, 1, 2) if forward else (2, 0, 1):
            weight_copy(e, i, weights[3 * e + i]).start()
        if not forward:
            act_copy(e).start()
    slot_tables(index_ref, table_ref, onehot, factor, ranks, blocks, cap)
    for copy, group in zip(copies_in, groups):
        copy.wait()
        pick_rows(buffer, onehot, rows, group, cap)

    @pl.loop(0, 2)
    def _(e):
        (forward_expert if forward else backward_expert)(
            e, rows, factor, gates.at[e], ups.at[e], downs.at[e],
            lambda i: weight_copy(e, i).wait(), acts.at[e], act_copy(e), hidden,
        )

    copies_out = [pltpu.make_async_copy(window(i), outs[i], in_sem.at[i]) for i in range(count)]
    for copy, group in zip(copies_out, groups):
        put_rows(buffer, onehot, rows, group, cap)
        copy.start()
    for copy in copies_out:
        copy.wait()
    if forward:
        for e in range(2):
            act_copy(e).wait()


def run_experts(forward, index, table, ins, weights, acts, cap):
    width, ff, tok = ins[0].shape[1], weights[0].shape[1], table.shape[2]
    groups, blocks = [], 0
    for value in ins:
        groups.append(list(range(blocks, blocks + value.shape[0] // tok)))
        blocks += value.shape[0] // tok
    slots = blocks * cap
    kept = jax.ShapeDtypeStruct((2, 2, slots, ff), BF16)
    out_shape = [jax.ShapeDtypeStruct(value.shape, BF16) for value in ins] + ([kept] if forward else [])
    in_place = pl.BlockSpec(memory_space=pl.ANY)
    operands = [index, table, *ins, *weights] + ([] if forward else [acts])
    return pl.pallas_call(
        functools.partial(experts_kernel, forward, cap, groups),
        out_shape=out_shape,
        in_specs=[pl.BlockSpec(memory_space=pltpu.SMEM), pl.BlockSpec(memory_space=pltpu.VMEM)]
        + [in_place] * (len(operands) - 2),
        out_specs=[in_place] * len(out_shape),
        scratch_shapes=[
            pltpu.VMEM((blocks * tok, width), BF16),
            pltpu.VMEM((2, slots, width), BF16),
            pltpu.VMEM((blocks, 2 * cap, tok), BF16),
            pltpu.VMEM((2, slots, tok), F32),
            pltpu.VMEM((2 * blocks, tok), F32),
            pltpu.VMEM((2, width, ff), BF16),
            pltpu.VMEM((2, width, ff), BF16),
            pltpu.VMEM((2, ff, width), BF16),
            pltpu.VMEM((2, 2, slots, ff), BF16),
            pltpu.VMEM((1 if forward else 2, slots, ff), BF16),
            pltpu.SemaphoreType.DMA((len(ins),)),
            pltpu.SemaphoreType.DMA((6,)),
            pltpu.SemaphoreType.DMA((2,)),
        ],
        compiler_params=pltpu.CompilerParams(vmem_limit_bytes=58 << 20),
        cost_estimate=pl.CostEstimate(
            flops=2 * 2 * 3 * slots * width * ff,
            bytes_accessed=2 * (6 * width * ff + 2 * blocks * tok * width) + 8 * slots * ff,
            transcendentals=2 * slots * ff,
        ),
    )(*operands)


def ep_permute(value, partner):
    return lax.ppermute(value, "ep", [(i, partner(i)) for i in range(8)])


def first(value):
    return ep_permute(value, lambda i: i ^ (4 if i & 1 else 2))


def second(value):
    return ep_permute(value, lambda i: i ^ (2 if i & 1 else 4))


def along_z(value, k):
    return lax.ppermute(value, "seq", [(i, i ^ k) for i in range(4)])


def add(*values):
    total = values[0].astype(F32)
    for value in values[1:]:
        total = total + value.astype(F32)
    return total


ORDER = (
    ("g0a", ()), ("x0a", ()), ("x2z", ()), ("x1z", ()), ("w0", ()), ("x0b", ("g0a",)), ("g0b", ("w0", "x0a",)),
    ("w2", ("w0", "x0a", "g0a",)), ("w1", ("w2",)), ("x3z", ("w2",)), ("x1a", ("x2z", "w2",)),
    ("x2a", ("w1", "x1z",)), ("x1b", ("w1", "x1z", "x2z",)), ("g2z", ("x3z", "x0b", "w1", "x1z",)),
    ("tab", ("g0b", "x3z", "x0b", "w1", "x1z",)), ("x3a", ("x1a", "g0b", "x0b", "w1",)),
    ("x2b", ("x1a", "g0b", "x3z", "x0b",)), ("x3b", ("x2a",)), ("g2a", ("x3a", "x2a",)),
    ("g3z", ("x3a", "x2a",)), ("g1z", ("x1b", "x2b", "g2z", "x3a",)), ("g2b", ("x1b", "x2b",)), ("F", ()),
    ("o1a", ("g2b",)), ("g3a", ("F", "g1z", "g2b",)), ("o3b", ("g1z", "g2b", "g3z",)),
    ("g1b", ("F", "g1z", "g2b", "g3z",)), ("o1z", ()), ("g3b", ("o1a",)), ("o3a", ("g3a", "o1a",)),
    ("g1a", ("o3b", "g3a", "o1a",)), ("o2b", ("o1z", "o3b", "g3a",)), ("o1b", ("g1b", "o1z", "o3b", "g3a",)),
    ("o3z", ("g3b", "g1b", "o1z",)), ("B", ("o3a", "o1z",)), ("o2a", ("B",)), ("d3b", ()), ("d2b", ()),
    ("d1b", ()), ("o2z", ()), ("d3a", ()), ("d1a", ()), ("d2a", ()), ("d3z", ()), ("d0b", ()), ("o0b", ()),
    ("d2z", ()), ("d1z", ()), ("d0a", ()), ("o0a", ()),
)


def gathered(tokens, expert_ids, route_weights, norm_gain, gate_proj, up_proj, down_proj, out_grad):
    experts = lax.axis_size("seq") * lax.axis_size("ep")
    tok, fanout = expert_ids.shape
    cap = max(2, 3 * tok * fanout // (2 * experts))
    mine = (gate_proj[0], up_proj[0], down_proj[0])
    ids = jnp.arange(experts, dtype=jnp.int32)
    routes = jnp.sum(
        jnp.where(expert_ids[:, :, None] == ids[None, None, :], route_weights[:, :, None], 0.0), axis=1
    )
    pairs = routes.T.reshape(experts // 2, 2, tok)
    for_device = jnp.stack([pairs, pairs[:, ::-1]], axis=1).reshape(experts, 2 * tok)
    x_float = tokens.astype(F32)
    normed = scale_rows(x_float, norm_gain).astype(BF16)
    z, ep = lax.axis_index("seq"), lax.axis_index("ep")
    core = ep % 2
    step_first = jnp.where(core == 1, 4, 2)
    step_second = jnp.where(core == 1, 2, 4)
    masks = [0, step_first, step_second, step_first | step_second]
    done = {"x0": normed, "g0": out_grad}

    def experts_pass(forward, offsets, source, target, acts, wait):
        keys = [(k, s) for k in offsets for s in "0ab"]
        blocks = [(k, j) for k, s in keys for j in ((2, 3) if s == "b" else ("0a".index(s),))]
        index = jnp.stack([(z ^ k) * 8 + (ep ^ masks[j]) for k, j in blocks]).astype(jnp.int32)
        arrays = [done[source + ("0" if (k, s) == (0, "0") else f"{k}z" if s == "0" else f"{k}{s}")] for k, s in keys]
        theirs = tuple(done[f"w{i}"] for i in range(3))
        table = done["tab"].reshape(experts, 2, tok)
        out = run_experts(forward, wait(index), table, arrays, mine + theirs, acts, cap)
        for (k, s), value in zip(keys, out):
            done[f"{target}part{k}{s}"] = value
        return out

    def spread_step(name, wait):
        t, k, move = name[0], int(name[1]), name[2]
        own = done[f"{t}0"]
        if move == "z":
            return along_z(wait(done[f"{t}2z"]), 1) if k == 3 else along_z(wait(own), k)
        if name[1:] == "1b":
            return along_z(wait(done[f"{t}0b"]), 1)
        shard = own if k == 0 else done[f"{t}{k}z"]
        if move == "a":
            return first(wait(shard))
        return second(jnp.concatenate([shard, wait(done[f"{t}{k}a"])], axis=0))

    def merge_step(name, wait):
        t, k, move = name[0], int(name[1]), name[2]

        def part(s):
            return done[f"{t}part{k}{s}"]

        if name[1:] == "1b":
            return along_z(wait(part("b")), 1)
        if move == "b":
            value = add(part("b"), done[f"{t}1b"]).astype(BF16) if k == 0 else part("b")
            return second(wait(value))
        if move == "a":
            value = part("a") if k == 1 else add(part("a"), done[f"{t}{k}b"][tok:]).astype(BF16)
            return first(wait(value))
        value = total(t, k)
        return along_z(wait(value.astype(BF16)), 2 if k == 2 else 1)

    def total(t, k):
        values = [done[f"{t}part{k}0"], done[f"{t}{k}a"]]
        if k != 1:
            values.append(done[f"{t}{k}b"][:tok])
        if k == 2:
            values.append(done[f"{t}3z"])
        if k == 0:
            values += [done[f"{t}1z"], done[f"{t}2z"]]
        return add(*values)

    acts = {}
    for name, others in ORDER:

        def wait(value, others=others):
            if not others:
                return value
            return lax.optimization_barrier((value, *[done[n] for n in others]))[0]

        with jax.named_scope(name):
            if name[0] in "FB":
                offsets = {"0": (0, 2), "1": (1, 3)}.get(name[1:], (0, 1, 2, 3))
                if name[0] == "F":
                    out = experts_pass(True, offsets, "x", "o", None, wait)
                    acts[offsets] = out[-1]
                else:
                    out = experts_pass(False, offsets, "g", "d", acts[offsets], wait)
                done[name] = out[0]
            elif name == "tab":
                done[name] = lax.all_to_all(wait(for_device), ("seq", "ep"), split_axis=0, concat_axis=0, tiled=True)
            elif name[0] == "w":
                done[name] = ep_permute(wait(mine[int(name[1])]), lambda i: i ^ 1)
            else:
                done[name] = (spread_step if name[0] in "xg" else merge_step)(name, wait)
    return (total("o", 0).astype(BF16), norm_grad(x_float, norm_gain, total("d", 0)))


def expert_forward(inputs, gate_w, up_w, down_w):
    gate_act = jnp.dot(inputs, gate_w, preferred_element_type=jnp.float32)
    upward = jnp.dot(inputs, up_w, preferred_element_type=jnp.float32)
    hidden = (jax.nn.silu(gate_act) * upward).astype(jnp.bfloat16)
    result = jnp.dot(hidden, down_w, preferred_element_type=jnp.float32).astype(jnp.bfloat16)
    return (result, gate_act, upward)


def expert_backward(grads, gate_act, upward, gate_w, up_w, down_w):
    pairs = (((1,), (1,)), ((), ()))
    grad_hidden = lax.dot_general(grads, down_w, pairs, preferred_element_type=jnp.float32)
    sigmoid_gate = jax.nn.sigmoid(gate_act)
    grad_gate = (
        grad_hidden * upward * sigmoid_gate * (1.0 + gate_act * (1.0 - sigmoid_gate))
    ).astype(jnp.bfloat16)
    grad_up = (grad_hidden * (gate_act * sigmoid_gate)).astype(jnp.bfloat16)
    summed = lax.dot_general(grad_gate, gate_w, pairs, preferred_element_type=jnp.float32)
    summed = summed + lax.dot_general(grad_up, up_w, pairs, preferred_element_type=jnp.float32)
    return summed.astype(jnp.bfloat16)


def move_out(slots):
    arrived = lax.all_to_all(slots, ("seq", "ep"), split_axis=0, concat_axis=0, tiled=True)
    return arrived


def move_back(slots):
    arrived = lax.all_to_all(slots, ("seq", "ep"), split_axis=0, concat_axis=0, tiled=True)
    return arrived


def run_live(compute, inputs):
    outputs = list(compute(inputs))
    return outputs


def exchanged(tokens, expert_ids, route_weights, norm_gain, gate_proj, up_proj, down_proj, out_grad):
    own_weights = (gate_proj[0], up_proj[0], down_proj[0])
    experts = lax.axis_size("seq") * lax.axis_size("ep")
    tok_count, fanout = expert_ids.shape
    model_width = tokens.shape[1]
    capacity = max(2, 3 * tok_count * fanout // (2 * experts))
    zero_value = jnp.zeros((), jnp.bfloat16)
    x_float = tokens.astype(jnp.float32)
    normed = scale_rows(x_float, norm_gain).astype(jnp.bfloat16)
    flat_ids = expert_ids.reshape(-1)
    one_hot = (flat_ids[:, None] == jnp.arange(experts, dtype=jnp.int32)[None, :]).astype(jnp.int32)
    slot_rank = jnp.sum((jnp.cumsum(one_hot, axis=0) - one_hot) * one_hot, axis=1)
    groups = [(0, capacity, own_weights)]
    position = flat_ids * capacity + slot_rank
    slot_route = (
        jnp.full((experts * capacity,), -1, jnp.int32)
        .at[position]
        .set(jnp.arange(flat_ids.shape[0], dtype=jnp.int32))
    )
    alive_slot = slot_route >= 0
    source = jnp.maximum(slot_route, 0) // fanout
    outgoing = jnp.where(alive_slot[:, None], normed[source], zero_value).reshape(
        experts, capacity, model_width
    )
    arrived = move_out(outgoing)
    first, width, weight_set = groups[0]
    inputs = arrived.reshape(-1, model_width)
    alive_rows = jnp.any(inputs != 0, axis=1)

    def forward_pass(parts, weight_set=weight_set):
        return expert_forward(parts[0], *weight_set)

    result, gate_act, upward = run_live(forward_pass, [inputs])
    saved = [(gate_act, upward, alive_rows)]
    result_parts = result.reshape(experts, width, model_width)
    route_out = move_back(result_parts).reshape(-1, model_width)[position]
    outgoing_grad = jnp.where(alive_slot[:, None], out_grad[source], zero_value).reshape(
        experts, capacity, model_width
    )
    grads_arrived = move_out(outgoing_grad)
    grad_parts = []
    for (first, width, weight_set), (gate_act, upward, alive_rows) in zip(groups, saved):
        grads = grads_arrived.reshape(-1, model_width)

        def backward_pass(parts, weight_set=weight_set):
            return (expert_backward(parts[0], parts[1], parts[2], *weight_set),)

        grad_rows = run_live(backward_pass, [grads, gate_act, upward])[0]
        grad_parts.append(grad_rows.reshape(experts, width, model_width))
    route_grad = move_back(grad_parts[0]).reshape(-1, model_width)[position]
    weight_cube = route_weights[:, :, None]
    moe_out = jnp.sum(
        weight_cube * route_out.reshape(tok_count, fanout, model_width).astype(jnp.float32), axis=1
    ).astype(jnp.bfloat16)
    grad_normed = jnp.sum(
        weight_cube * route_grad.reshape(tok_count, fanout, model_width).astype(jnp.float32), axis=1
    )

    def normalize(values):
        return scale_rows(values, norm_gain)

    _, pullback = jax.vjp(normalize, x_float)
    in_grad = pullback(grad_normed)[0].astype(jnp.bfloat16)
    return (moe_out, in_grad)


def solution(mesh):
    rows = P(("seq", "ep"), None)
    cubes = P(("seq", "ep"), None, None)
    planes = mesh.shape["seq"] == 4 and mesh.shape["ep"] == 8
    return jax.shard_map(
        gathered if planes else exchanged,
        mesh=mesh,
        in_specs=(rows, rows, rows, P(), cubes, cubes, cubes, rows),
        out_specs=(rows, rows),
        check_vma=False,
    )
```
